512 devices in a mesh: mem: 16 (over z_hi, y), reg: 32 (over x, z_lo, core).
Axes of the slice: x: 4, y: 8, z: 8 (z_hi: 2, z_lo: 4; z = z_hi * 4 + z_lo), core: 2. Of those that a mesh axis runs over, the one named last changes fastest.
Arguments:
- ensemble: float32 [256, 131072], P('mem', 'reg'), may hold values from -6 to 6
- obs_pert: float32 [256, 32768], P('mem', 'reg'), may hold values from -45 to 45
- innovation: float32 [32768], P('reg'), may hold values from -6 to 6
- block_list: int32 [512, 8], P(('reg', 'mem')), may hold values from 0 to 255, as said below
- loc_weights: float32 [512, 8, 128], P(('reg', 'mem')), may hold values from 0.05 to 1
Outputs:
- analysis: float32 [256, 131072], P('mem', 'reg')
The draws below stay inside these ranges and needn't reach their ends.
Inputs may be any that keep to these rules, and one draw needn't show every extreme that they name: `block_list`: each patch lists 8 different blocks. The regions split the patches and the blocks each into equal runs in order; a patch lists only blocks of its own region and of the regions just before and after it, and always the first and the last block of its own region.
All inputs are finite; a program needn't handle non-finite values.
Results may differ from the reference program's by a relative error of at most 0.0003.
Values sent between devices are 32-bit elements; how exact they have to be, the bound alone decides.
No kernel may reach another device: no remote copies, remote signals or barrier semaphores. Data moves between devices by JAX's collectives and lax.ppermute only.
A program may use at most 64 MiB of HBM per device.

```python
import math
import jax
import jax.numpy as jnp
from jax import lax

MEMBERS = 256
PATCH = 256
OBS_BLOCK = 128
BLOCKS_PATCH = 8
NEWTON = 8
BLK_REG = 8
PATCHES = 512
POINTS = 131072
BLOCKS = 256
OBS = 32768


def draw_obs_pert(key, part):
    noise_draw = jnp.clip(jax.random.normal(jax.random.fold_in(key, 11), (MEMBERS, OBS), jnp.float32), -5.0, 5.0)
    log_lower = math.log(0.3)
    log_upper = math.log(3.0)
    member_scale = jnp.exp(jax.random.uniform(jax.random.fold_in(key, 12), (MEMBERS, 1), jnp.float32, log_lower, log_upper))
    obs_scale = jnp.exp(jax.random.uniform(jax.random.fold_in(key, 13), (1, OBS), jnp.float32, log_lower, log_upper))
    return jnp.clip(noise_draw * member_scale * obs_scale, -45.0, 45.0)


def draw_block_list(key, part):
    regions = BLOCKS // BLK_REG
    patch_ids = jnp.arange(PATCHES, dtype=jnp.int32)
    region = patch_ids // (PATCHES // regions)
    candidates = jnp.arange(3 * BLK_REG, dtype=jnp.int32)
    global_ids = (region[:, None] - 1) * BLK_REG + candidates[None, :]
    is_valid = (global_ids >= 0) & (global_ids < BLOCKS)
    raw_score = jax.random.randint(jax.random.fold_in(key, 21), (PATCHES, 3 * BLK_REG), 0, 1 << 20, jnp.int32)
    scores = raw_score * (3 * BLK_REG) + candidates[None, :]
    forced = (candidates == BLK_REG) | (candidates == 2 * BLK_REG - 1)
    scores = jnp.where(forced[None, :], (1 << 30) + candidates[None, :], scores)
    scores = jnp.where(is_valid, scores, -1 - candidates[None, :])
    unused_values, picked = lax.top_k(scores, BLOCKS_PATCH)
    chosen = jnp.take_along_axis(global_ids, picked, axis=1)
    return chosen.astype(jnp.int32)


def steps_of(stream_key, extent, pieces, least, top_value):
    def one(axis_at, parts):
        heights = jax.random.uniform(jax.random.fold_in(jax.random.fold_in(stream_key, 6), axis_at), (parts,), jnp.float32, least / len(pieces), top_value / len(pieces))
        return jnp.repeat(jnp.exp(heights), extent[axis_at] // parts).reshape((-1,) + (1,) * (len(extent) - axis_at - 1))

    factor_of = one(*pieces[0])
    for cut in pieces[1:]:
        factor_of = factor_of * one(*cut)
    return factor_of


def bell_draw(own_key, extent, scale, most, shards=(), kind=jnp.bfloat16):
    values = jax.random.normal(own_key, extent, jnp.float32) * scale
    if len(shards) > 0:
        values = steps_of(own_key, extent, shards, -0.22, 0.18) * values
    return jnp.clip(values, min=-most, max=most).astype(kind)


def setup_inputs(seed: int = 0) -> dict:
    streams_of = jax.random.split(jax.random.key(seed), 6)
    ensemble = bell_draw(streams_of[0], (MEMBERS, POINTS), 1.0, 6.0, ((0, 16), (1, 32)), jnp.float32)
    obs_pert = draw_obs_pert(jax.random.fold_in(streams_of[5], 71), 0)
    innovation = bell_draw(streams_of[2], (OBS,), 1.0, 6.0, ((0, 32),), jnp.float32)
    block_list = draw_block_list(jax.random.fold_in(streams_of[5], 71), 0)
    loc_weights = jnp.clip(0.05 + 0.95 * jax.random.uniform(streams_of[4], (PATCHES, BLOCKS_PATCH, OBS_BLOCK), jnp.float32) ** steps_of(streams_of[4], (PATCHES, BLOCKS_PATCH, OBS_BLOCK), ((0, 512),), -0.2, 0.2), 0.05, 1.0)
    return dict(ensemble=ensemble, obs_pert=obs_pert, innovation=innovation, block_list=block_list, loc_weights=loc_weights)


def batched(first, second, form):
    return jnp.einsum(form, first, second, precision=lax.Precision.HIGHEST, preferred_element_type=jnp.float32)

def analyse(columns, blocks, innov_blocks, weights):
    members = columns.shape[0]
    ens_mean = lax.optimization_barrier(jnp.mean(columns, axis=0))
    anomalies = columns - ens_mean[None]
    weighted = blocks * weights[None]
    gram_matrix = batched(weighted, blocks, 'kpo,jpo->pkj')
    drive = batched(weighted, innov_blocks, 'kpo,po->pk')
    identity = jnp.eye(members, dtype=jnp.float32)
    system = identity[None] + gram_matrix / (members - 1.0)
    trace_sum = jnp.trace(system, axis1=1, axis2=2)
    iterate_y = system / trace_sum[:, None, None]
    iterate_z = jnp.broadcast_to(identity[None], system.shape)
    for repeat in range(NEWTON):
        factor = 1.5 * identity[None] - 0.5 * batched(iterate_z, iterate_y, 'pij,pjk->pik')
        iterate_y, iterate_z = (batched(iterate_y, factor, 'pij,pjk->pik'), batched(factor, iterate_z, 'pij,pjk->pik'))
    root = iterate_z / jnp.sqrt(trace_sum)[:, None, None]
    half_step = batched(root, drive, 'pij,pj->pi')
    mean_weights = batched(root, half_step, 'pij,pj->pi') / (members - 1.0)
    transform = root + mean_weights[:, :, None]
    return ens_mean[None] + batched(transform, anomalies, 'pkj,kps->jps')

def reference(ensemble, obs_pert, innovation, block_list, loc_weights):
    members = ensemble.shape[0]
    blocks_all = obs_pert.reshape(members, BLOCKS, OBS_BLOCK)
    innov_all = innovation.reshape(BLOCKS, OBS_BLOCK)

    def one_patch(index):
        columns = lax.dynamic_slice_in_dim(ensemble, index * PATCH, PATCH, 1).reshape(members, 1, PATCH)
        chosen = lax.dynamic_slice_in_dim(block_list, index, 1, 0)
        blocks = jnp.take(blocks_all, chosen, axis=1).reshape(members, 1, BLOCKS_PATCH * OBS_BLOCK)
        innov_blocks = jnp.take(innov_all, chosen, axis=0).reshape(1, BLOCKS_PATCH * OBS_BLOCK)
        weights = lax.dynamic_slice_in_dim(loc_weights, index, 1, 0).reshape(1, BLOCKS_PATCH * OBS_BLOCK)
        return analyse(columns, blocks, innov_blocks, weights)[:, 0, :]
    result = lax.map(one_patch, jnp.arange(PATCHES, dtype=jnp.int32))
    return jnp.transpose(result, (1, 0, 2)).reshape(members, PATCHES * PATCH)
```

```python
import jax
import jax.numpy as jnp
from jax import lax
from jax.experimental import pallas as pl
from jax.experimental.pallas import tpu as pltpu
from jax.sharding import PartitionSpec as P

NEWTON = 8
F32 = jnp.float32
BF16 = jnp.bfloat16
VMEM = pltpu.VMEM


def whole(count):
    return [pl.BlockSpec(memory_space=VMEM)] * count


def pack(ensemble, block_list):
    rows, columns = ensemble.shape
    groups = lax.axis_size("mem")
    width = columns // groups
    halves = width // 128
    depth = halves * rows + 8

    def kernel(ens_ref, list_ref, out_ref):
        tile = jnp.broadcast_to(list_ref[...], (8, 128))
        for patch in range(groups):
            for half in range(halves):
                start = patch * width + half * 128
                out_ref[patch * depth + half * rows : patch * depth + (half + 1) * rows, :] = ens_ref[
                    :, start : start + 128
                ]
            out_ref[patch * depth + halves * rows : (patch + 1) * depth, :] = tile

    listed = jnp.pad(block_list.astype(F32), ((0, 0), (0, 128 - block_list.shape[1])))
    return pl.pallas_call(
        kernel,
        out_shape=jax.ShapeDtypeStruct((groups * depth, 128), F32),
        in_specs=whole(2),
        out_specs=pl.BlockSpec(memory_space=VMEM),
        name="pack",
    )(ensemble, listed)


def select(lists, left, own, right, rows):
    patches = lists.shape[0] - 1
    per_patch = lists.shape[1]
    obs = own.shape[1]
    blocks = obs // 128

    def kernel(lists_ref, left_ref, own_ref, right_ref, out_ref, innov_ref, table, innov_table):
        for side, ref in enumerate((left_ref, own_ref, right_ref)):
            for block in range(blocks):
                at = side * blocks + block
                table[at] = ref[0:rows, block * 128 : (block + 1) * 128]
                innov_table[at] = ref[rows : rows + 1, block * 128 : (block + 1) * 128]
        for patch in range(patches):
            for slot in range(per_patch):
                out_ref[patch * rows : (patch + 1) * rows, slot * 128 : (slot + 1) * 128] = table[
                    lists_ref[patch, slot]
                ]
        for slot in range(per_patch):
            innov_ref[slot : slot + 1, :] = innov_table[lists_ref[patches, slot]]

    return pl.pallas_call(
        kernel,
        out_shape=(
            jax.ShapeDtypeStruct((patches * rows, per_patch * 128), F32),
            jax.ShapeDtypeStruct((per_patch, 128), F32),
        ),
        grid_spec=pltpu.PrefetchScalarGridSpec(
            num_scalar_prefetch=1,
            grid=(),
            in_specs=whole(3),
            out_specs=whole(2),
            scratch_shapes=[
                pltpu.VMEM((3 * blocks, rows, 128), F32),
                pltpu.VMEM((3 * blocks, 1, 128), F32),
            ],
        ),
        name="select",
    )(lists, left, own, right)


def parts(value):
    high = value.astype(BF16)
    return high, (value - high.astype(F32)).astype(BF16)


def product(first, second):
    high1, low1 = first
    high2, low2 = second
    dot = lambda a, b: jnp.dot(a, b, preferred_element_type=F32)
    return dot(high1, high2) + (dot(high1, low2) + dot(low1, high2))


def analyse(obs, innov, weights, packed, rows):
    members, count = obs.shape
    slots = innov.shape[0]
    depth = packed.shape[0] // (members // rows)
    halves = (depth - 8) // rows
    width = halves * 128
    groups = members // rows

    def kernel(obs_ref, innov_ref, weights_ref, packed_ref, out_ref, columns):
        for group in range(groups):
            for half in range(halves):
                columns[group * rows : (group + 1) * rows, half * 128 : (half + 1) * 128] = packed_ref[
                    group * depth + half * rows : group * depth + (half + 1) * rows, :
                ]
        root_weights = jnp.sqrt(weights_ref[...])
        gram_matrix = jnp.zeros((members, members), F32)
        cross = jnp.zeros((members, members), F32)
        drive = jnp.zeros((members, 128), F32)
        contract = lambda a, b: lax.dot_general(
            a, b, (((1,), (1,)), ((), ())), preferred_element_type=F32
        )
        for slot in range(slots):
            scaled = obs_ref[:, slot * 128 : (slot + 1) * 128] * root_weights[slot : slot + 1, :]
            drive += scaled * (root_weights[slot : slot + 1, :] * innov_ref[slot : slot + 1, :])
            high, low = parts(scaled)
            gram_matrix += contract(high, high)
            cross += contract(high, low)
        gram_matrix += cross + cross.T
        drive = jnp.sum(drive, axis=1, keepdims=True)
        identity = (
            lax.broadcasted_iota(jnp.int32, (members, members), 0)
            == lax.broadcasted_iota(jnp.int32, (members, members), 1)
        ).astype(F32)
        system = identity + gram_matrix / (members - 1.0)
        trace_sum = jnp.sum(system * identity, keepdims=True)
        iterate_y = system / trace_sum
        half_three = 1.5 * identity
        factor = half_three - 0.5 * iterate_y
        y_parts = parts(iterate_y)
        z_parts = parts(factor)
        y_parts = parts(product(y_parts, z_parts))
        for repeat in range(1, NEWTON):
            factor = parts(half_three - 0.5 * product(z_parts, y_parts))
            iterate_z = product(factor, z_parts)
            if repeat < NEWTON - 1:
                y_parts = parts(product(y_parts, factor))
                z_parts = parts(iterate_z)
        root = iterate_z / jnp.sqrt(trace_sum)
        half_step = jnp.sum(root * drive, axis=0, keepdims=True)
        mean_weights = jnp.sum(root * half_step, axis=1, keepdims=True) / (members - 1.0)
        ens = columns[...]
        ens_mean = jnp.mean(ens, axis=0, keepdims=True)
        anomalies = ens - ens_mean
        shift = ens_mean + jnp.sum(mean_weights * anomalies, axis=0, keepdims=True)
        out_ref[...] = product(parts(root), parts(anomalies)) + shift

    return pl.pallas_call(
        kernel,
        out_shape=jax.ShapeDtypeStruct((members, width), F32),
        in_specs=whole(4),
        out_specs=pl.BlockSpec(memory_space=VMEM),
        scratch_shapes=[pltpu.VMEM((members, width), F32)],
        name="analyse",
    )(obs, innov, weights, packed)


def on_device(ensemble, obs_pert, innovation, block_list, loc_weights):
    groups = lax.axis_size("mem")
    regions = lax.axis_size("reg")
    rows, own_obs = obs_pert.shape
    weights = loc_weights.reshape(loc_weights.shape[1:])
    slots, block_size = weights.shape
    own_blocks = own_obs // block_size

    packed = lax.all_to_all(pack(ensemble, block_list), "mem", split_axis=0, concat_axis=0, tiled=True)
    table = jnp.concatenate([obs_pert, innovation.reshape(1, own_obs)], axis=0)
    left = lax.ppermute(table, "reg", [(i, i + 1) for i in range(regions - 1)])
    right = lax.ppermute(table, "reg", [(i + 1, i) for i in range(regions - 1)])

    depth = packed.shape[0] // groups
    lists = packed.reshape(groups, depth, 128)[:, depth - 1, :slots].astype(jnp.int32)
    offset = (lax.axis_index("reg") - 1) * own_blocks
    lists = jnp.concatenate([lists, block_list], axis=0) - offset
    chosen, innov = select(lists, left, table, right, rows)
    obs = lax.all_to_all(chosen, "mem", split_axis=0, concat_axis=0, tiled=True)
    updated = analyse(obs, innov, weights, packed, rows)
    sent = lax.all_to_all(updated, "mem", split_axis=0, concat_axis=0, tiled=True)
    return sent.reshape(groups, rows, -1).transpose(1, 0, 2).reshape(rows, -1)


def solution(mesh):
    return jax.shard_map(
        on_device,
        mesh=mesh,
        in_specs=(
            P("mem", "reg"),
            P("mem", "reg"),
            P("reg"),
            P(("reg", "mem"), None),
            P(("reg", "mem"), None, None),
        ),
        out_specs=P("mem", "reg"),
        check_vma=False,
    )
```

```python
import jax
import jax.numpy as jnp
from jax import lax
from jax.experimental import pallas as pl
from jax.experimental.pallas import tpu as pltpu
from jax.sharding import Mesh
from jax.sharding import PartitionSpec as P

NEWTON = 8
LANES = 128
TILE = 8
HALVES = 2
F32 = jnp.float32
BF16 = jnp.bfloat16
I32 = jnp.int32
MEM = ("half", "ring")


def whole(count):
    return [pl.BlockSpec(memory_space=pltpu.VMEM)] * count


def pack(ensemble, block_list):
    rows, columns = ensemble.shape
    slots = block_list.shape[1]
    groups = lax.axis_size(MEM)
    width = columns // groups
    pieces = width // LANES
    depth = pieces * rows + TILE

    def kernel(ens_ref, list_ref, out_ref, tile_ref):
        tile_ref[...] = jnp.zeros_like(tile_ref)
        tile_ref[0:1, 0:slots] = list_ref[...].astype(F32)
        tile = tile_ref[...]
        for patch in range(groups):
            base = patch * depth
            for piece in range(pieces):
                start = patch * width + piece * LANES
                out_ref[base + piece * rows : base + (piece + 1) * rows, :] = ens_ref[:, start : start + LANES]
            out_ref[base + pieces * rows : base + depth, :] = tile

    return pl.pallas_call(
        kernel,
        out_shape=jax.ShapeDtypeStruct((groups * depth, LANES), F32),
        in_specs=whole(2),
        out_specs=pl.BlockSpec(memory_space=pltpu.VMEM),
        scratch_shapes=[pltpu.VMEM((TILE, LANES), F32)],
        name="pack",
    )(ensemble, block_list)


def select(place, packed, block_list, left, own, right):
    members = own.shape[0] - 1
    obs = own.shape[1]
    blocks = obs // LANES
    slots = block_list.shape[1]
    ring = lax.axis_size("ring")
    groups = HALVES * ring
    depth = packed.shape[0] // groups

    def kernel(
        place_ref, packed_ref, list_ref, left_ref, own_ref, right_ref, out_ref, innov_ref, table, innov_table, lists, wanted, sem
    ):
        half = place_ref[0]
        offset = place_ref[1]
        for source in range(ring):
            at = pl.multiple_of((half * ring + source) * depth + depth - TILE, TILE)
            lists[source : source + 1, :] = packed_ref[pl.ds(at, TILE), :][0:1, :].astype(I32) - offset
        lists[ring : ring + 1, 0:slots] = list_ref[...] - offset
        copy = pltpu.make_async_copy(lists, wanted, sem)
        copy.start()
        for side, ref in enumerate((left_ref, own_ref, right_ref)):
            for block in range(blocks):
                at = side * blocks + block
                table[at] = ref[0:members, block * LANES : (block + 1) * LANES]
                innov_table[at] = ref[members : members + 1, block * LANES : (block + 1) * LANES]
        copy.wait()
        for patch in range(ring):
            for slot in range(slots):
                out_ref[patch * members : (patch + 1) * members, slot * LANES : (slot + 1) * LANES] = table[
                    wanted[patch, slot]
                ]
        for slot in range(slots):
            innov_ref[slot : slot + 1, :] = innov_table[wanted[ring, slot]]

    return pl.pallas_call(
        kernel,
        out_shape=(
            jax.ShapeDtypeStruct((ring * members, slots * LANES), F32),
            jax.ShapeDtypeStruct((slots, LANES), F32),
        ),
        in_specs=[pl.BlockSpec(memory_space=pltpu.SMEM)] + whole(5),
        out_specs=tuple(whole(2)),
        scratch_shapes=[
            pltpu.VMEM((3 * blocks, members, LANES), F32),
            pltpu.VMEM((3 * blocks, 1, LANES), F32),
            pltpu.VMEM((2 * TILE, LANES), I32),
            pltpu.SMEM((2 * TILE, LANES), I32),
            pltpu.SemaphoreType.DMA,
        ],
        name="select",
    )(place, packed, block_list, left, own, right)


def parts(value):
    high = value.astype(BF16)
    return high, (value - high.astype(F32)).astype(BF16)


def product(first, second):
    high1, low1 = first
    high2, low2 = second
    dot = lambda a, b: jnp.dot(a, b, preferred_element_type=F32)
    return dot(high1, high2) + (dot(high1, low2) + dot(low1, high2))


def analyse(place, obs, innov, weights, packed, rows):
    members, count = obs.shape
    slots = innov.shape[0]
    groups = members // rows
    ring = groups // HALVES
    depth = packed.shape[0] // groups
    pieces = (depth - TILE) // rows
    width = pieces * LANES

    def kernel(place_ref, obs_ref, innov_ref, weights_ref, packed_ref, out_ref, columns):
        half = place_ref[0]

        def member_group(chunk):
            return (half ^ (chunk % HALVES)) * ring + chunk // HALVES

        for chunk in range(groups):
            base = member_group(chunk) * depth
            for piece in range(pieces):
                at = pl.multiple_of(base + piece * rows, TILE)
                columns[chunk * rows : (chunk + 1) * rows, piece * LANES : (piece + 1) * LANES] = packed_ref[
                    pl.ds(at, rows), :
                ]
        root_weights = jnp.sqrt(weights_ref[...])
        gram_matrix = jnp.zeros((members, members), F32)
        cross = jnp.zeros((members, members), F32)
        drive = jnp.zeros((members, LANES), F32)
        contract = lambda a, b: lax.dot_general(
            a, b, (((1,), (1,)), ((), ())), preferred_element_type=F32
        )
        for slot in range(slots):
            scaled = obs_ref[:, slot * LANES : (slot + 1) * LANES] * root_weights[slot : slot + 1, :]
            drive += scaled * (root_weights[slot : slot + 1, :] * innov_ref[slot : slot + 1, :])
            high, low = parts(scaled)
            gram_matrix += contract(high, high)
            cross += contract(high, low)
        gram_matrix += cross + cross.T
        drive = jnp.sum(drive, axis=1, keepdims=True)
        identity = (
            lax.broadcasted_iota(I32, (members, members), 0) == lax.broadcasted_iota(I32, (members, members), 1)
        ).astype(F32)
        system = identity + gram_matrix / (members - 1.0)
        trace_sum = jnp.sum(system * identity, keepdims=True)
        iterate_y = system / trace_sum
        half_three = 1.5 * identity
        factor = half_three - 0.5 * iterate_y
        y_parts = parts(iterate_y)
        z_parts = parts(factor)
        y_parts = parts(product(y_parts, z_parts))
        for repeat in range(1, NEWTON):
            factor = parts(half_three - 0.5 * product(z_parts, y_parts))
            iterate_z = product(factor, z_parts)
            if repeat < NEWTON - 1:
                y_parts = parts(product(y_parts, factor))
                z_parts = parts(iterate_z)
        root = iterate_z / jnp.sqrt(trace_sum)
        half_step = jnp.sum(root * drive, axis=0, keepdims=True)
        mean_weights = jnp.sum(root * half_step, axis=1, keepdims=True) / (members - 1.0)
        ens = columns[...]
        ens_mean = jnp.mean(ens, axis=0, keepdims=True)
        anomalies = ens - ens_mean
        shift = ens_mean + jnp.sum(mean_weights * anomalies, axis=0, keepdims=True)
        updated = product(parts(root), parts(anomalies)) + shift
        for chunk in range(groups):
            at = pl.multiple_of(member_group(chunk) * rows, TILE)
            out_ref[pl.ds(at, rows), :] = updated[chunk * rows : (chunk + 1) * rows, :]

    return pl.pallas_call(
        kernel,
        out_shape=jax.ShapeDtypeStruct((members, width), F32),
        in_specs=[pl.BlockSpec(memory_space=pltpu.SMEM)] + whole(4),
        out_specs=pl.BlockSpec(memory_space=pltpu.VMEM),
        scratch_shapes=[pltpu.VMEM((members, width), F32)],
        name="analyse",
    )(place, obs, innov, weights, packed)


def on_device(ensemble, obs_pert, innovation, block_list, loc_weights):
    regions = lax.axis_size("reg")
    rows, own_obs = obs_pert.shape
    weights = loc_weights.reshape(loc_weights.shape[1:])
    block_size = weights.shape[1]
    own_blocks = own_obs // block_size
    place = jnp.stack([lax.axis_index("half"), (lax.axis_index("reg") - 1) * own_blocks]).astype(I32)

    partner = lax.ppermute(obs_pert, "half", [(0, 1), (1, 0)])
    packed = lax.all_to_all(pack(ensemble, block_list), MEM, split_axis=0, concat_axis=0, tiled=True)
    table = jnp.concatenate([obs_pert, partner, innovation.reshape(1, own_obs)], axis=0)
    left = lax.ppermute(table, "reg", [(i, i + 1) for i in range(regions - 1)])
    right = lax.ppermute(table, "reg", [(i + 1, i) for i in range(regions - 1)])
    chosen, innov = select(place, packed, block_list, left, table, right)
    obs = lax.all_to_all(chosen, "ring", split_axis=0, concat_axis=0, tiled=True)
    updated = analyse(place, obs, innov, weights, packed, rows)
    sent = lax.all_to_all(updated, MEM, split_axis=0, concat_axis=0, tiled=True)
    return sent.reshape(sent.shape[0] // rows, rows, -1).transpose(1, 0, 2).reshape(rows, -1)


def solution(mesh):
    groups, regions = (mesh.shape[name] for name in ("mem", "reg"))
    fine = Mesh(mesh.devices.reshape(HALVES, groups // HALVES, regions), MEM + ("reg",))
    return jax.shard_map(
        on_device,
        mesh=fine,
        in_specs=(
            P(MEM, "reg"),
            P(MEM, "reg"),
            P("reg"),
            P(("reg",) + MEM, None),
            P(("reg",) + MEM, None, None),
        ),
        out_specs=P(MEM, "reg"),
        check_vma=False,
    )
```

```python
import jax
import jax.numpy as jnp
from jax import lax
from jax.experimental import pallas as pl
from jax.experimental.pallas import tpu as pltpu
from jax.sharding import Mesh
from jax.sharding import PartitionSpec as P


NEWTON = 8
LANES = 128
TILE = 8
HALVES = 2
F32 = jnp.float32
BF16 = jnp.bfloat16
I32 = jnp.int32
MEM = ("half", "ring")


def whole(count):
    return [pl.BlockSpec(memory_space=pltpu.VMEM)] * count


def near(*arrays):
    return [pltpu.with_memory_space_constraint(value, pltpu.VMEM) for value in arrays]


def pack(ensemble, block_list):
    rows, columns = ensemble.shape
    slots = block_list.shape[1]
    groups = lax.axis_size(MEM)
    width = columns // groups
    pieces = width // LANES
    depth = pieces * rows + TILE

    def kernel(ens_ref, list_ref, out_ref, tile_ref):
        tile_ref[...] = jnp.zeros_like(tile_ref)
        tile_ref[0:1, 0:slots] = list_ref[...].astype(F32)
        tile = tile_ref[...]
        for patch in range(groups):
            base = patch * depth
            for piece in range(pieces):
                start = patch * width + piece * LANES
                out_ref[base + piece * rows : base + (piece + 1) * rows, :] = ens_ref[:, start : start + LANES]
            out_ref[base + pieces * rows : base + depth, :] = tile

    return pl.pallas_call(
        kernel,
        out_shape=pltpu.VMEM((groups * depth, LANES), F32),
        in_specs=whole(2),
        out_specs=pl.BlockSpec(memory_space=pltpu.VMEM),
        scratch_shapes=[pltpu.VMEM((TILE, LANES), F32)],
        name="pack",
    )(ensemble, block_list)


def select(packed, block_list, left, own, right):
    members = own.shape[0] - 1
    obs = own.shape[1]
    blocks = obs // LANES
    slots = block_list.shape[1]
    ring = lax.axis_size("ring")
    groups = HALVES * ring
    depth = packed.shape[0] // groups

    def kernel(
        packed_ref, list_ref, left_ref, own_ref, right_ref, out_ref, innov_ref, table, innov_table, lists, wanted, sem
    ):
        half = lax.axis_index("half")
        offset = (lax.axis_index("reg") - 1) * blocks
        for source in range(ring):
            at = pl.multiple_of((half * ring + source) * depth + depth - TILE, TILE)
            lists[source : source + 1, :] = packed_ref[pl.ds(at, TILE), :][0:1, :].astype(I32) - offset
        lists[ring : ring + 1, 0:slots] = list_ref[...] - offset
        copy = pltpu.make_async_copy(lists, wanted, sem)
        copy.start()
        for side, ref in enumerate((left_ref, own_ref, right_ref)):
            for block in range(blocks):
                at = side * blocks + block
                table[at] = ref[0:members, block * LANES : (block + 1) * LANES]
                innov_table[at] = ref[members : members + 1, block * LANES : (block + 1) * LANES]
        copy.wait()
        for patch in range(ring):
            for slot in range(slots):
                out_ref[patch * members : (patch + 1) * members, slot * LANES : (slot + 1) * LANES] = table[
                    wanted[patch, slot]
                ]
        for slot in range(slots):
            innov_ref[slot : slot + 1, :] = innov_table[wanted[ring, slot]]

    return pl.pallas_call(
        kernel,
        out_shape=(
            pltpu.VMEM((ring * members, slots * LANES), F32),
            pltpu.VMEM((slots, LANES), F32),
        ),
        in_specs=whole(5),
        out_specs=tuple(whole(2)),
        scratch_shapes=[
            pltpu.VMEM((3 * blocks, members, LANES), F32),
            pltpu.VMEM((3 * blocks, 1, LANES), F32),
            pltpu.VMEM((2 * TILE, LANES), I32),
            pltpu.SMEM((2 * TILE, LANES), I32),
            pltpu.SemaphoreType.DMA,
        ],
        name="select",
    )(*near(packed), block_list, *near(left, own, right))


def parts(value):
    high = value.astype(BF16)
    return high, (value - high.astype(F32)).astype(BF16)


def product(first, second):
    high1, low1 = first
    high2, low2 = second
    dot = lambda a, b: jnp.dot(a, b, preferred_element_type=F32)
    return dot(high1, high2) + (dot(high1, low2) + dot(low1, high2))


def analyse(obs, innov, weights, packed, rows):
    members, _ = obs.shape
    slots = innov.shape[0]
    groups = members // rows
    ring = groups // HALVES
    depth = packed.shape[0] // groups
    pieces = (depth - TILE) // rows
    width = pieces * LANES

    def kernel(obs_ref, innov_ref, weights_ref, packed_ref, out_ref, columns):
        half = lax.axis_index("half")

        def member_group(chunk):
            return (half ^ (chunk % HALVES)) * ring + chunk // HALVES

        for chunk in range(groups):
            base = member_group(chunk) * depth
            for piece in range(pieces):
                at = pl.multiple_of(base + piece * rows, TILE)
                columns[chunk * rows : (chunk + 1) * rows, piece * LANES : (piece + 1) * LANES] = packed_ref[
                    pl.ds(at, rows), :
                ]
        root_weights = jnp.sqrt(weights_ref[...])
        gram_matrix = jnp.zeros((members, members), F32)
        cross = jnp.zeros((members, members), F32)
        drive = jnp.zeros((members, LANES), F32)
        contract = lambda a, b: lax.dot_general(
            a, b, (((1,), (1,)), ((), ())), preferred_element_type=F32
        )
        for slot in range(slots):
            scaled = obs_ref[:, slot * LANES : (slot + 1) * LANES] * root_weights[slot : slot + 1, :]
            drive += scaled * (root_weights[slot : slot + 1, :] * innov_ref[slot : slot + 1, :])
            high, low = parts(scaled)
            gram_matrix += contract(high, high)
            cross += contract(high, low)
        gram_matrix += cross + cross.T
        drive = jnp.sum(drive, axis=1, keepdims=True)
        identity = (
            lax.broadcasted_iota(I32, (members, members), 0) == lax.broadcasted_iota(I32, (members, members), 1)
        ).astype(F32)
        system = identity + gram_matrix / (members - 1.0)
        trace_sum = jnp.sum(system * identity, keepdims=True)
        iterate_y = system / trace_sum
        half_three = 1.5 * identity
        factor = half_three - 0.5 * iterate_y
        y_parts = parts(iterate_y)
        z_parts = parts(factor)
        y_parts = parts(product(y_parts, z_parts))
        for repeat in range(1, NEWTON):
            factor = parts(half_three - 0.5 * product(z_parts, y_parts))
            iterate_z = product(factor, z_parts)
            if repeat < NEWTON - 1:
                y_parts = parts(product(y_parts, factor))
                z_parts = parts(iterate_z)
        root = iterate_z / jnp.sqrt(trace_sum)
        half_step = jnp.sum(root * drive, axis=0, keepdims=True)
        mean_weights = jnp.sum(root * half_step, axis=1, keepdims=True) / (members - 1.0)
        ens = columns[...]
        ens_mean = jnp.mean(ens, axis=0, keepdims=True)
        anomalies = ens - ens_mean
        shift = ens_mean + jnp.sum(mean_weights * anomalies, axis=0, keepdims=True)
        updated = product(parts(root), parts(anomalies)) + shift
        for chunk in range(groups):
            at = pl.multiple_of(member_group(chunk) * rows, TILE)
            out_ref[pl.ds(at, rows), :] = updated[chunk * rows : (chunk + 1) * rows, :]

    return pl.pallas_call(
        kernel,
        out_shape=pltpu.VMEM((members, width), F32),
        in_specs=whole(4),
        out_specs=pl.BlockSpec(memory_space=pltpu.VMEM),
        scratch_shapes=[pltpu.VMEM((members, width), F32)],
        name="analyse",
    )(*near(obs, innov), weights, *near(packed))


def on_device(ensemble, obs_pert, innovation, block_list, loc_weights):
    regions = lax.axis_size("reg")
    rows, own_obs = obs_pert.shape
    weights = loc_weights.reshape(loc_weights.shape[1:])

    partner = lax.ppermute(obs_pert, "half", [(0, 1), (1, 0)])
    packed = pack(ensemble, block_list)
    packed = lax.all_to_all(packed, MEM, split_axis=0, concat_axis=0, tiled=True)
    table = jnp.concatenate([obs_pert, partner, innovation.reshape(1, own_obs)], axis=0)
    left = lax.ppermute(table, "reg", [(i, i + 1) for i in range(regions - 1)])
    right = lax.ppermute(table, "reg", [(i + 1, i) for i in range(regions - 1)])
    chosen, innov = select(packed, block_list, left, table, right)
    obs = lax.all_to_all(chosen, "ring", split_axis=0, concat_axis=0, tiled=True)
    updated = analyse(obs, innov, weights, packed, rows)
    sent = lax.all_to_all(updated, MEM, split_axis=0, concat_axis=0, tiled=True)
    return sent.reshape(sent.shape[0] // rows, rows, -1).transpose(1, 0, 2).reshape(rows, -1)


def solution(mesh):
    groups, regions = (mesh.shape[name] for name in ("mem", "reg"))
    fine = Mesh(mesh.devices.reshape(HALVES, groups // HALVES, regions), MEM + ("reg",))
    return jax.shard_map(
        on_device,
        mesh=fine,
        in_specs=(
            P(MEM, "reg"),
            P(MEM, "reg"),
            P("reg"),
            P(("reg",) + MEM, None),
            P(("reg",) + MEM, None, None),
        ),
        out_specs=P(MEM, "reg"),
        check_vma=False,
    )
```

```python
import jax
import jax.numpy as jnp
from jax import lax
from jax.experimental import pallas as pl
from jax.experimental.pallas import tpu as pltpu
from jax.sharding import Mesh
from jax.sharding import PartitionSpec as P


NEWTON = 8
LANES = 128
TILE = 8
HALVES = 2
F32 = jnp.float32
BF16 = jnp.bfloat16
I32 = jnp.int32
MEM = ("half", "ring")


def whole(count):
    return [pl.BlockSpec(memory_space=pltpu.VMEM)] * count


def near(*arrays):
    return [pltpu.with_memory_space_constraint(value, pltpu.VMEM) for value in arrays]


def pack(ensemble, block_list):
    rows, columns = ensemble.shape
    slots = block_list.shape[1]
    ring = lax.axis_size("ring")
    width = columns // (HALVES * ring)
    pieces = width // LANES
    depth = HALVES * pieces * rows + TILE

    def kernel(ens_ref, list_ref, out_ref):
        half = lax.axis_index("half")
        for target in range(ring):
            at = target * depth
            for other in range(HALVES):
                patch = (half ^ other) * ring + target
                for piece in range(pieces):
                    start = pl.multiple_of(patch * width + piece * LANES, LANES)
                    out_ref[at : at + rows, :] = ens_ref[:, pl.ds(start, LANES)]
                    at += rows
            out_ref[at : at + TILE, :] = jnp.zeros((TILE, LANES), F32)
            out_ref[at : at + 1, 0:slots] = list_ref[...].astype(F32)

    return pl.pallas_call(
        kernel,
        out_shape=pltpu.VMEM((ring * depth, LANES), F32),
        in_specs=whole(2),
        out_specs=pl.BlockSpec(memory_space=pltpu.VMEM),
        name="pack",
    )(ensemble, block_list)


def select(listed, block_list, left, own, right):
    members = own.shape[0] - 1
    obs = own.shape[1]
    blocks = obs // LANES
    slots = block_list.shape[1]
    ring = lax.axis_size("ring")
    depth = listed.shape[0] // ring

    def kernel(
        listed_ref, list_ref, left_ref, own_ref, right_ref, out_ref, innov_ref, table, innov_table, lists, wanted, sem
    ):
        offset = (lax.axis_index("reg") - 1) * blocks
        for source in range(ring):
            at = (source + 1) * depth - TILE
            lists[source : source + 1, :] = listed_ref[at : at + 1, :].astype(I32) - offset
        lists[ring : ring + 1, 0:slots] = list_ref[...] - offset
        copy = pltpu.make_async_copy(lists, wanted, sem)
        copy.start()
        for side, ref in enumerate((left_ref, own_ref, right_ref)):
            for block in range(blocks):
                at = side * blocks + block
                table[at] = ref[0:members, block * LANES : (block + 1) * LANES]
                innov_table[at] = ref[members : members + 1, block * LANES : (block + 1) * LANES]
        copy.wait()
        for patch in range(ring):
            for slot in range(slots):
                out_ref[patch * members : (patch + 1) * members, slot * LANES : (slot + 1) * LANES] = table[
                    wanted[patch, slot]
                ]
        for slot in range(slots):
            innov_ref[slot : slot + 1, :] = innov_table[wanted[ring, slot]]

    return pl.pallas_call(
        kernel,
        out_shape=(
            pltpu.VMEM((ring * members, slots * LANES), F32),
            pltpu.VMEM((slots, LANES), F32),
        ),
        in_specs=whole(5),
        out_specs=tuple(whole(2)),
        scratch_shapes=[
            pltpu.VMEM((3 * blocks, members, LANES), F32),
            pltpu.VMEM((3 * blocks, 1, LANES), F32),
            pltpu.VMEM((2 * TILE, LANES), I32),
            pltpu.SMEM((2 * TILE, LANES), I32),
            pltpu.SemaphoreType.DMA,
        ],
        name="select",
    )(*near(listed), block_list, *near(left, own, right))


def parts(value):
    high = value.astype(BF16)
    return high, (value - high.astype(F32)).astype(BF16)


def product(first, second):
    high1, low1 = first
    high2, low2 = second
    dot = lambda a, b: jnp.dot(a, b, preferred_element_type=F32)
    return dot(high1, high2) + (dot(high1, low2) + dot(low1, high2))


def analyse(obs, innov, weights, packed, crossed, rows):
    members, _ = obs.shape
    slots = innov.shape[0]
    groups = members // rows
    ring = groups // HALVES
    depth = packed.shape[0] // ring
    pieces = (depth - TILE) // (HALVES * rows)
    width = pieces * LANES

    def kernel(obs_ref, innov_ref, weights_ref, packed_ref, crossed_ref, out_ref, columns):
        half = lax.axis_index("half")
        for source in range(ring):
            for piece in range(pieces):
                lanes = slice(piece * LANES, (piece + 1) * LANES)
                own = source * depth + piece * rows
                other = (source * pieces + piece) * rows
                at = HALVES * source * rows
                columns[at : at + rows, lanes] = packed_ref[own : own + rows, :]
                columns[at + rows : at + HALVES * rows, lanes] = crossed_ref[other : other + rows, :]
        root_weights = jnp.sqrt(weights_ref[...])
        gram_matrix = jnp.zeros((members, members), F32)
        cross = jnp.zeros((members, members), F32)
        drive = jnp.zeros((members, LANES), F32)
        contract = lambda a, b: lax.dot_general(
            a, b, (((1,), (1,)), ((), ())), preferred_element_type=F32
        )
        for slot in range(slots):
            scaled = obs_ref[:, slot * LANES : (slot + 1) * LANES] * root_weights[slot : slot + 1, :]
            drive += scaled * (root_weights[slot : slot + 1, :] * innov_ref[slot : slot + 1, :])
            high, low = parts(scaled)
            gram_matrix += contract(high, high)
            cross += contract(high, low)
        gram_matrix += cross + cross.T
        drive = jnp.sum(drive, axis=1, keepdims=True)
        identity = (
            lax.broadcasted_iota(I32, (members, members), 0) == lax.broadcasted_iota(I32, (members, members), 1)
        ).astype(F32)
        system = identity + gram_matrix / (members - 1.0)
        trace_sum = jnp.sum(system * identity, keepdims=True)
        iterate_y = system / trace_sum
        half_three = 1.5 * identity
        factor = half_three - 0.5 * iterate_y
        y_parts = parts(iterate_y)
        z_parts = parts(factor)
        y_parts = parts(product(y_parts, z_parts))
        for repeat in range(1, NEWTON):
            factor = parts(half_three - 0.5 * product(z_parts, y_parts))
            iterate_z = product(factor, z_parts)
            if repeat < NEWTON - 1:
                y_parts = parts(product(y_parts, factor))
                z_parts = parts(iterate_z)
        root = iterate_z / jnp.sqrt(trace_sum)
        half_step = jnp.sum(root * drive, axis=0, keepdims=True)
        mean_weights = jnp.sum(root * half_step, axis=1, keepdims=True) / (members - 1.0)
        ens = columns[...]
        ens_mean = jnp.mean(ens, axis=0, keepdims=True)
        anomalies = ens - ens_mean
        shift = ens_mean + jnp.sum(mean_weights * anomalies, axis=0, keepdims=True)
        updated = product(parts(root), parts(anomalies)) + shift
        for chunk in range(groups):
            group = (half ^ (chunk % HALVES)) * ring + chunk // HALVES
            at = pl.multiple_of(group * rows, TILE)
            out_ref[pl.ds(at, rows), :] = updated[chunk * rows : (chunk + 1) * rows, :]

    return pl.pallas_call(
        kernel,
        out_shape=pltpu.VMEM((members, width), F32),
        in_specs=whole(5),
        out_specs=pl.BlockSpec(memory_space=pltpu.VMEM),
        scratch_shapes=[pltpu.VMEM((members, width), F32)],
        name="analyse",
    )(*near(obs, innov), weights, *near(packed, crossed))


def on_device(ensemble, obs_pert, innovation, block_list, loc_weights):
    regions = lax.axis_size("reg")
    rows, own_obs = obs_pert.shape
    weights = loc_weights.reshape(loc_weights.shape[1:])

    partner = lax.ppermute(obs_pert, "half", [(0, 1), (1, 0)])
    packed = pack(ensemble, block_list)
    packed = lax.all_to_all(packed, "ring", split_axis=0, concat_axis=0, tiled=True)
    table = jnp.concatenate([obs_pert, partner, innovation.reshape(1, own_obs)], axis=0)
    left = lax.ppermute(table, "reg", [(i, i + 1) for i in range(regions - 1)])
    right = lax.ppermute(table, "reg", [(i + 1, i) for i in range(regions - 1)])
    chosen, innov = select(packed, block_list, left, table, right)
    obs = lax.all_to_all(chosen, "ring", split_axis=0, concat_axis=0, tiled=True)
    ring = lax.axis_size("ring")
    chunks = packed.reshape(ring, -1, LANES)
    part = (chunks.shape[1] - TILE) // HALVES
    crossed = lax.ppermute(chunks[:, part : 2 * part, :].reshape(-1, LANES), "half", [(0, 1), (1, 0)])
    updated = analyse(obs, innov, weights, packed, crossed, rows)
    sent = lax.all_to_all(updated, MEM, split_axis=0, concat_axis=0, tiled=True)
    return sent.reshape(sent.shape[0] // rows, rows, -1).transpose(1, 0, 2).reshape(rows, -1)


def solution(mesh):
    groups, regions = (mesh.shape[name] for name in ("mem", "reg"))
    fine = Mesh(mesh.devices.reshape(HALVES, groups // HALVES, regions), MEM + ("reg",))
    return jax.shard_map(
        on_device,
        mesh=fine,
        in_specs=(
            P(MEM, "reg"),
            P(MEM, "reg"),
            P("reg"),
            P(("reg",) + MEM, None),
            P(("reg",) + MEM, None, None),
        ),
        out_specs=P(MEM, "reg"),
        check_vma=False,
    )
```

```python
import jax
import jax.numpy as jnp
from jax import lax
from jax.experimental import pallas as pl
from jax.experimental.pallas import tpu as pltpu
from jax.sharding import Mesh
from jax.sharding import PartitionSpec as P


NEWTON = 8
LANES = 128
TILE = 8
HALVES = 2
F32 = jnp.float32
BF16 = jnp.bfloat16
I32 = jnp.int32
MEM = ("half", "ring")


def whole(count):
    return [pl.BlockSpec(memory_space=pltpu.VMEM)] * count


def near(*arrays):
    return [pltpu.with_memory_space_constraint(value, pltpu.VMEM) for value in arrays]


def pack(ensemble, block_list):
    rows, columns = ensemble.shape
    slots = block_list.shape[1]
    ring = lax.axis_size("ring")
    width = columns // (HALVES * ring)
    pieces = width // LANES
    depth = HALVES * pieces * rows + TILE

    def kernel(ens_ref, list_ref, out_ref):
        half = lax.axis_index("half")
        for target in range(ring):
            at = target * depth
            for other in range(HALVES):
                patch = (half ^ other) * ring + target
                for piece in range(pieces):
                    start = pl.multiple_of(patch * width + piece * LANES, LANES)
                    out_ref[at : at + rows, :] = ens_ref[:, pl.ds(start, LANES)]
                    at += rows
            out_ref[at : at + TILE, :] = jnp.zeros((TILE, LANES), F32)
            out_ref[at : at + 1, 0:slots] = list_ref[...].astype(F32)

    return pl.pallas_call(
        kernel,
        out_shape=pltpu.VMEM((ring * depth, LANES), F32),
        in_specs=whole(2),
        out_specs=pl.BlockSpec(memory_space=pltpu.VMEM),
        name="pack",
    )(*near(ensemble), block_list)


def select(listed, block_list, own, near_side, far_side):
    members = own.shape[0] - 1
    obs = own.shape[1]
    blocks = obs // LANES
    slots = block_list.shape[1]
    ring = lax.axis_size("ring")
    depth = listed.shape[0] // ring

    def kernel(
        listed_ref, list_ref, own_ref, near_ref, far_ref, out_ref, innov_ref, table, innov_table, lists, wanted, sem
    ):
        region = lax.axis_index("reg")
        offset = (region - 1) * blocks
        odd = lax.rem(region, 2)
        for source in range(ring):
            at = (source + 1) * depth - TILE
            lists[source : source + 1, :] = listed_ref[at : at + 1, :].astype(I32) - offset
        lists[ring : ring + 1, 0:slots] = list_ref[...] - offset
        copy = pltpu.make_async_copy(lists, wanted, sem)
        copy.start()
        for side, ref in ((1, own_ref), (2 - 2 * odd, near_ref), (2 * odd, far_ref)):
            for block in range(blocks):
                at = side * blocks + block
                table[at] = ref[0:members, block * LANES : (block + 1) * LANES]
                innov_table[at] = ref[members : members + 1, block * LANES : (block + 1) * LANES]
        copy.wait()
        for patch in range(ring):
            for slot in range(slots):
                out_ref[patch * members : (patch + 1) * members, slot * LANES : (slot + 1) * LANES] = table[
                    wanted[patch, slot]
                ]
        for slot in range(slots):
            innov_ref[slot : slot + 1, :] = innov_table[wanted[ring, slot]]

    return pl.pallas_call(
        kernel,
        out_shape=(
            pltpu.VMEM((ring * members, slots * LANES), F32),
            pltpu.VMEM((slots, LANES), F32),
        ),
        in_specs=whole(5),
        out_specs=tuple(whole(2)),
        scratch_shapes=[
            pltpu.VMEM((3 * blocks, members, LANES), F32),
            pltpu.VMEM((3 * blocks, 1, LANES), F32),
            pltpu.VMEM((2 * TILE, LANES), I32),
            pltpu.SMEM((2 * TILE, LANES), I32),
            pltpu.SemaphoreType.DMA,
        ],
        name="select",
    )(*near(listed), block_list, *near(own, near_side, far_side))


def parts(value):
    high = value.astype(BF16)
    return high, (value - high.astype(F32)).astype(BF16)


def product(first, second):
    high1, low1 = first
    high2, low2 = second
    dot = lambda a, b: jnp.dot(a, b, preferred_element_type=F32)
    return dot(high1, high2) + (dot(high1, low2) + dot(low1, high2))


def analyse(obs, innov, weights, packed, crossed, rows):
    members, _ = obs.shape
    slots = innov.shape[0]
    groups = members // rows
    ring = groups // HALVES
    depth = packed.shape[0] // ring
    pieces = (depth - TILE) // (HALVES * rows)
    width = pieces * LANES

    def kernel(obs_ref, innov_ref, weights_ref, packed_ref, crossed_ref, out_ref, columns):
        half = lax.axis_index("half")
        for source in range(ring):
            for piece in range(pieces):
                lanes = slice(piece * LANES, (piece + 1) * LANES)
                own = source * depth + piece * rows
                other = (source * pieces + piece) * rows
                at = HALVES * source * rows
                columns[at : at + rows, lanes] = packed_ref[own : own + rows, :]
                columns[at + rows : at + HALVES * rows, lanes] = crossed_ref[other : other + rows, :]
        root_weights = jnp.sqrt(weights_ref[...])
        gram_matrix = jnp.zeros((members, members), F32)
        cross = jnp.zeros((members, members), F32)
        drive = jnp.zeros((members, LANES), F32)
        contract = lambda a, b: lax.dot_general(
            a, b, (((1,), (1,)), ((), ())), preferred_element_type=F32
        )
        for slot in range(slots):
            scaled = obs_ref[:, slot * LANES : (slot + 1) * LANES] * root_weights[slot : slot + 1, :]
            drive += scaled * (root_weights[slot : slot + 1, :] * innov_ref[slot : slot + 1, :])
            high, low = parts(scaled)
            gram_matrix += contract(high, high)
            cross += contract(high, low)
        gram_matrix += cross + cross.T
        drive = jnp.sum(drive, axis=1, keepdims=True)
        identity = (
            lax.broadcasted_iota(I32, (members, members), 0) == lax.broadcasted_iota(I32, (members, members), 1)
        ).astype(F32)
        system = identity + gram_matrix / (members - 1.0)
        trace_sum = jnp.sum(system * identity, keepdims=True)
        iterate_y = system / trace_sum
        half_three = 1.5 * identity
        factor = half_three - 0.5 * iterate_y
        y_parts = parts(iterate_y)
        z_parts = parts(factor)
        y_parts = parts(product(y_parts, z_parts))
        for repeat in range(1, NEWTON):
            factor = parts(half_three - 0.5 * product(z_parts, y_parts))
            iterate_z = product(factor, z_parts)
            if repeat < NEWTON - 1:
                y_parts = parts(product(y_parts, factor))
                z_parts = parts(iterate_z)
        root = iterate_z / jnp.sqrt(trace_sum)
        half_step = jnp.sum(root * drive, axis=0, keepdims=True)
        mean_weights = jnp.sum(root * half_step, axis=1, keepdims=True) / (members - 1.0)
        ens = columns[...]
        ens_mean = jnp.mean(ens, axis=0, keepdims=True)
        anomalies = ens - ens_mean
        shift = ens_mean + jnp.sum(mean_weights * anomalies, axis=0, keepdims=True)
        updated = product(parts(root), parts(anomalies)) + shift
        for chunk in range(groups):
            group = (half ^ (chunk % HALVES)) * ring + chunk // HALVES
            at = pl.multiple_of(group * rows, TILE)
            out_ref[pl.ds(at, rows), :] = updated[chunk * rows : (chunk + 1) * rows, :]

    return pl.pallas_call(
        kernel,
        out_shape=pltpu.VMEM((members, width), F32),
        in_specs=whole(5),
        out_specs=pl.BlockSpec(memory_space=pltpu.VMEM),
        scratch_shapes=[pltpu.VMEM((members, width), F32)],
        name="analyse",
    )(*near(obs, innov), weights, *near(packed, crossed))


def on_device(ensemble, obs_pert, innovation, block_list, loc_weights):
    regions = lax.axis_size("reg")
    rows, own_obs = obs_pert.shape
    weights = loc_weights.reshape(loc_weights.shape[1:])

    partner = lax.ppermute(obs_pert, "half", [(0, 1), (1, 0)])
    packed = pack(ensemble, block_list)
    packed = lax.all_to_all(packed, "ring", split_axis=0, concat_axis=0, tiled=True)
    table = jnp.concatenate([obs_pert, partner, innovation.reshape(1, own_obs)], axis=0)
    swaps = [[(i + a, i + 1 - a) for i in range(first, regions - 1, 2) for a in (0, 1)] for first in (0, 1)]
    far_side = lax.ppermute(table, "reg", swaps[1])
    near_side = lax.ppermute(table, "reg", swaps[0])
    chosen, innov = select(packed, block_list, table, near_side, far_side)
    obs = lax.all_to_all(chosen, "ring", split_axis=0, concat_axis=0, tiled=True)
    ring = lax.axis_size("ring")
    chunks = packed.reshape(ring, -1, LANES)
    part = (chunks.shape[1] - TILE) // HALVES
    crossed = lax.ppermute(chunks[:, part : 2 * part, :].reshape(-1, LANES), "half", [(0, 1), (1, 0)])
    updated = analyse(obs, innov, weights, packed, crossed, rows)
    sent = lax.all_to_all(updated, MEM, split_axis=0, concat_axis=0, tiled=True)
    return sent.reshape(sent.shape[0] // rows, rows, -1).transpose(1, 0, 2).reshape(rows, -1)


def solution(mesh):
    groups, regions = (mesh.shape[name] for name in ("mem", "reg"))
    fine = Mesh(mesh.devices.reshape(HALVES, groups // HALVES, regions), MEM + ("reg",))
    return jax.shard_map(
        on_device,
        mesh=fine,
        in_specs=(
            P(MEM, "reg"),
            P(MEM, "reg"),
            P("reg"),
            P(("reg",) + MEM, None),
            P(("reg",) + MEM, None, None),
        ),
        out_specs=P(MEM, "reg"),
        check_vma=False,
    )
```

```python
import jax
import jax.numpy as jnp
from jax import lax
from jax.experimental import pallas as pl
from jax.experimental.pallas import tpu as pltpu
from jax.sharding import Mesh
from jax.sharding import PartitionSpec as P


NEWTON = 8
LANES = 128
TILE = 8
HALVES = 2
FIXED = 2
F32 = jnp.float32
BF16 = jnp.bfloat16
I32 = jnp.int32
MEM = ("half", "ring")


def whole(count):
    return [pl.BlockSpec(memory_space=pltpu.VMEM)] * count


def near(*arrays):
    return [pltpu.with_memory_space_constraint(value, pltpu.VMEM) for value in arrays]


def pack(ensemble, obs_pert, block_list):
    rows, columns = ensemble.shape
    obs = obs_pert.shape[1]
    slots = block_list.shape[1]
    ring = lax.axis_size("ring")
    width = columns // (HALVES * ring)
    pieces = width // LANES
    depth = (HALVES * pieces + FIXED) * rows + TILE

    def kernel(ens_ref, obs_ref, list_ref, out_ref):
        half = lax.axis_index("half")
        for target in range(ring):
            at = target * depth
            for other in range(HALVES):
                patch = (half ^ other) * ring + target
                for piece in range(pieces):
                    start = pl.multiple_of(patch * width + piece * LANES, LANES)
                    out_ref[at : at + rows, :] = ens_ref[:, pl.ds(start, LANES)]
                    at += rows
            for start in (0, obs - LANES):
                out_ref[at : at + rows, :] = obs_ref[:, start : start + LANES]
                at += rows
            out_ref[at : at + TILE, :] = jnp.zeros((TILE, LANES), F32)
            out_ref[at : at + 1, 0:slots] = list_ref[...].astype(F32)

    return pl.pallas_call(
        kernel,
        out_shape=pltpu.VMEM((ring * depth, LANES), F32),
        in_specs=whole(3),
        out_specs=pl.BlockSpec(memory_space=pltpu.VMEM),
        name="pack",
    )(ensemble, obs_pert, block_list)


def select(listed, block_list, weights, own, near_side, far_side):
    members = own.shape[0] - 1
    blocks = own.shape[1] // LANES
    slots = block_list.shape[1]
    others = slots - FIXED
    ring = lax.axis_size("ring")
    depth = listed.shape[0] // ring
    fixed = (blocks, 2 * blocks - 1)

    def kernel(
        listed_ref, list_ref, weights_ref, own_ref, near_ref, far_ref, out_ref, scales_ref,
        table, innov_table, lists, staged, wanted, rest, list_sem, sems,
    ):
        region = lax.axis_index("reg")
        offset = (region - 1) * blocks
        odd = lax.rem(region, 2)
        for source in range(ring):
            at = (source + 1) * depth - TILE
            lists[source : source + 1, :] = listed_ref[at : at + 1, :].astype(I32) - offset
        lists[ring : ring + 1, 0:slots] = list_ref[...] - offset
        copy = pltpu.make_async_copy(lists, wanted, list_sem)
        copy.start()
        for side, ref in ((1, own_ref), (2 - 2 * odd, near_ref), (2 * odd, far_ref)):
            for block in range(blocks):
                at = side * blocks + block
                table[at] = ref[0:members, block * LANES : (block + 1) * LANES]
                innov_table[at] = ref[members : members + 1, block * LANES : (block + 1) * LANES]
        copy.wait()

        def compact(patch, order):
            count = jnp.int32(0)
            places = [jnp.int32(0)] * FIXED
            for slot in range(slots):
                block = wanted[patch, slot]
                rest[order, count] = block
                if order:
                    rest[2, count] = jnp.int32(slot)
                    places = [jnp.where(block == f, slot, at) for f, at in zip(fixed, places)]
                found = [block == f for f in fixed]
                count = count + jnp.where(found[0] | found[1], 0, 1)
            return places

        copies = []
        for patch in range(ring):
            compact(patch, 0)
            for slot in range(others):
                staged[patch * members : (patch + 1) * members, slot * LANES : (slot + 1) * LANES] = table[rest[0, slot]]
            span = pl.ds(patch * members, members)
            copies.append(pltpu.make_async_copy(staged.at[span], out_ref.at[span], sems.at[patch]))
            copies[-1].start()
        places = compact(ring, 1)
        for slot in range(others):
            scales_ref[slot : slot + 1, :] = innov_table[rest[1, slot]]
            scales_ref[slots + slot : slots + slot + 1, :] = weights_ref[pl.ds(rest[2, slot], 1), :]
        for which in range(FIXED):
            slot = others + which
            scales_ref[slot : slot + 1, :] = innov_table[fixed[which]]
            scales_ref[slots + slot : slots + slot + 1, :] = weights_ref[pl.ds(places[which], 1), :]
        for copy in copies:
            copy.wait()

    return pl.pallas_call(
        kernel,
        out_shape=(
            jax.ShapeDtypeStruct((ring * members, others * LANES), F32),
            pltpu.VMEM((2 * slots, LANES), F32),
        ),
        in_specs=whole(6),
        out_specs=(pl.BlockSpec(memory_space=pl.ANY), pl.BlockSpec(memory_space=pltpu.VMEM)),
        scratch_shapes=[
            pltpu.VMEM((3 * blocks, members, LANES), F32),
            pltpu.VMEM((3 * blocks, 1, LANES), F32),
            pltpu.VMEM((2 * TILE, LANES), I32),
            pltpu.VMEM((ring * members, others * LANES), F32),
            pltpu.SMEM((2 * TILE, LANES), I32),
            pltpu.SMEM((3, slots), I32),
            pltpu.SemaphoreType.DMA,
            pltpu.SemaphoreType.DMA((ring,)),
        ],
        name="select",
    )(*near(listed), block_list, *near(weights, own, near_side, far_side))


def parts(value):
    high = value.astype(BF16)
    return high, (value - high.astype(F32)).astype(BF16)


def product(first, second):
    high1, low1 = first
    high2, low2 = second
    dot = lambda a, b: jnp.dot(a, b, preferred_element_type=F32)
    return dot(high1, high2) + (dot(high1, low2) + dot(low1, high2))


def analyse(obs, scales, packed, crossed, rows):
    members, _ = obs.shape
    slots = scales.shape[0] // 2
    others = slots - FIXED
    groups = members // rows
    ring = groups // HALVES
    depth = packed.shape[0] // ring
    strips = crossed.shape[0] // (ring * rows)
    pieces = strips - FIXED
    width = pieces * LANES

    def kernel(obs_ref, scales_ref, packed_ref, crossed_ref, out_ref, columns):
        half = lax.axis_index("half")
        for source in range(ring):
            for strip in range(strips):
                lanes = slice(strip * LANES, (strip + 1) * LANES)
                skip = strip if strip < pieces else strip + pieces
                own = source * depth + skip * rows
                other = (source * strips + strip) * rows
                at = HALVES * source * rows
                columns[at : at + rows, lanes] = packed_ref[own : own + rows, :]
                columns[at + rows : at + HALVES * rows, lanes] = crossed_ref[other : other + rows, :]
        root_weights = jnp.sqrt(scales_ref[slots : 2 * slots, :])
        gram_matrix = jnp.zeros((members, members), F32)
        cross = jnp.zeros((members, members), F32)
        drive = jnp.zeros((members, LANES), F32)
        contract = lambda a, b: lax.dot_general(
            a, b, (((1,), (1,)), ((), ())), preferred_element_type=F32
        )
        for slot in range(slots):
            if slot < others:
                block = obs_ref[:, slot * LANES : (slot + 1) * LANES]
            else:
                block = columns[:, width + (slot - others) * LANES : width + (slot - others + 1) * LANES]
            scaled = block * root_weights[slot : slot + 1, :]
            drive += scaled * (root_weights[slot : slot + 1, :] * scales_ref[slot : slot + 1, :])
            high, low = parts(scaled)
            gram_matrix += contract(high, high)
            cross += contract(high, low)
        gram_matrix += cross + cross.T
        drive = jnp.sum(drive, axis=1, keepdims=True)
        identity = (
            lax.broadcasted_iota(I32, (members, members), 0) == lax.broadcasted_iota(I32, (members, members), 1)
        ).astype(F32)
        system = identity + gram_matrix / (members - 1.0)
        trace_sum = jnp.sum(system * identity, keepdims=True)
        iterate_y = system / trace_sum
        half_three = 1.5 * identity
        factor = half_three - 0.5 * iterate_y
        y_parts = parts(iterate_y)
        z_parts = parts(factor)
        y_parts = parts(product(y_parts, z_parts))
        for repeat in range(1, NEWTON):
            factor = parts(half_three - 0.5 * product(z_parts, y_parts))
            iterate_z = product(factor, z_parts)
            if repeat < NEWTON - 1:
                y_parts = parts(product(y_parts, factor))
                z_parts = parts(iterate_z)
        root = iterate_z / jnp.sqrt(trace_sum)
        half_step = jnp.sum(root * drive, axis=0, keepdims=True)
        mean_weights = jnp.sum(root * half_step, axis=1, keepdims=True) / (members - 1.0)
        ens = columns[:, 0:width]
        ens_mean = jnp.mean(ens, axis=0, keepdims=True)
        anomalies = ens - ens_mean
        shift = ens_mean + jnp.sum(mean_weights * anomalies, axis=0, keepdims=True)
        updated = product(parts(root), parts(anomalies)) + shift
        for chunk in range(groups):
            group = (half ^ (chunk % HALVES)) * ring + chunk // HALVES
            at = pl.multiple_of(group * rows, TILE)
            out_ref[pl.ds(at, rows), :] = updated[chunk * rows : (chunk + 1) * rows, :]

    return pl.pallas_call(
        kernel,
        out_shape=pltpu.VMEM((members, width), F32),
        in_specs=whole(4),
        out_specs=pl.BlockSpec(memory_space=pltpu.VMEM),
        scratch_shapes=[pltpu.VMEM((members, strips * LANES), F32)],
        name="analyse",
    )(*near(obs, scales, packed, crossed))


def on_device(ensemble, obs_pert, innovation, block_list, loc_weights):
    regions = lax.axis_size("reg")
    rows, own_obs = obs_pert.shape
    weights = loc_weights.reshape(loc_weights.shape[1:])

    partner = lax.ppermute(obs_pert, "half", [(0, 1), (1, 0)])
    packed = pack(ensemble, obs_pert, block_list)
    packed = lax.all_to_all(packed, "ring", split_axis=0, concat_axis=0, tiled=True)
    table = jnp.concatenate([obs_pert, partner, innovation.reshape(1, own_obs)], axis=0)
    swaps = [[(i + a, i + 1 - a) for i in range(first, regions - 1, 2) for a in (0, 1)] for first in (0, 1)]
    far_side = lax.ppermute(table, "reg", swaps[1])
    near_side = lax.ppermute(table, "reg", swaps[0])
    chosen, scales = select(packed, block_list, weights, table, near_side, far_side)
    obs = lax.all_to_all(chosen, "ring", split_axis=0, concat_axis=0, tiled=True)
    ring = lax.axis_size("ring")
    chunks = packed.reshape(ring, -1, LANES)
    part = ensemble.shape[1] // (HALVES * ring) // LANES * rows
    crossed = lax.ppermute(chunks[:, part : chunks.shape[1] - TILE, :].reshape(-1, LANES), "half", [(0, 1), (1, 0)])
    updated = analyse(obs, scales, packed, crossed, rows)
    sent = lax.all_to_all(updated, MEM, split_axis=0, concat_axis=0, tiled=True)
    return sent.reshape(sent.shape[0] // rows, rows, -1).transpose(1, 0, 2).reshape(rows, -1)


def solution(mesh):
    groups, regions = (mesh.shape[name] for name in ("mem", "reg"))
    fine = Mesh(mesh.devices.reshape(HALVES, groups // HALVES, regions), MEM + ("reg",))
    return jax.shard_map(
        on_device,
        mesh=fine,
        in_specs=(
            P(MEM, "reg"),
            P(MEM, "reg"),
            P("reg"),
            P(("reg",) + MEM, None),
            P(("reg",) + MEM, None, None),
        ),
        out_specs=P(MEM, "reg"),
        check_vma=False,
    )
```

```python
import jax
import jax.numpy as jnp
from jax import lax
from jax.experimental import pallas as pl
from jax.experimental.pallas import tpu as pltpu
from jax.sharding import Mesh
from jax.sharding import PartitionSpec as P


NEWTON = 8
LANES = 128
TILE = 8
HALVES = 2
FIXED = 2
F32 = jnp.float32
BF16 = jnp.bfloat16
I32 = jnp.int32
MEM = ("half", "ring")


def whole(count):
    return [pl.BlockSpec(memory_space=pltpu.VMEM)] * count


def near(*arrays):
    return [pltpu.with_memory_space_constraint(value, pltpu.VMEM) for value in arrays]


def pack(ensemble, obs_pert, block_list):
    rows, columns = ensemble.shape
    obs = obs_pert.shape[1]
    slots = block_list.shape[1]
    ring = lax.axis_size("ring")
    width = columns // (HALVES * ring)
    pieces = width // LANES
    depth = (HALVES * pieces + FIXED) * rows + TILE

    strips = HALVES * pieces + FIXED

    def kernel(ens_ref, obs_ref, list_ref, out_ref, listed, tile, list_sem, sems):
        half = lax.axis_index("half")
        fetch = pltpu.make_async_copy(list_ref, listed, list_sem)
        fetch.start()
        copies = []

        def send(source, at, size):
            copy = pltpu.make_async_copy(source, out_ref.at[at : at + size], sems.at[len(copies)])
            copy.start()
            copies.append(copy)

        for target in range(ring):
            at = target * depth
            for other in range(HALVES):
                patch = (half ^ other) * ring + target
                for piece in range(pieces):
                    start = pl.multiple_of(patch * width + piece * LANES, LANES)
                    send(ens_ref.at[:, pl.ds(start, LANES)], at, rows)
                    at += rows
            for start in (0, obs - LANES):
                send(obs_ref.at[:, start : start + LANES], at, rows)
                at += rows
        tile[...] = jnp.zeros_like(tile)
        fetch.wait()
        tile[0:1, 0:slots] = listed[...].astype(F32)
        for target in range(ring):
            send(tile, (target + 1) * depth - TILE, TILE)
        for copy in copies:
            copy.wait()

    return pl.pallas_call(
        kernel,
        out_shape=jax.ShapeDtypeStruct((ring * depth, LANES), F32),
        in_specs=[pl.BlockSpec(memory_space=pl.ANY)] * 3,
        out_specs=pl.BlockSpec(memory_space=pl.ANY),
        scratch_shapes=[
            pltpu.VMEM((1, slots), I32),
            pltpu.VMEM((TILE, LANES), F32),
            pltpu.SemaphoreType.DMA,
            pltpu.SemaphoreType.DMA((ring * (strips + 1),)),
        ],
        name="pack",
    )(ensemble, obs_pert, block_list)


def select(listed, slots, weights, own, near_side, far_side):
    members = own.shape[0] - 1
    blocks = own.shape[1] // LANES
    others = slots - FIXED
    ring = lax.axis_size("ring")
    depth = listed.shape[0] // ring
    fixed = (blocks, 2 * blocks - 1)

    def kernel(
        listed_ref, weights_ref, own_ref, near_ref, far_ref, out_ref, scales_ref,
        table, innov_table, lists, staged, wanted, rest, list_sem, sems,
    ):
        region = lax.axis_index("reg")
        offset = (region - 1) * blocks
        odd = lax.rem(region, 2)
        for source in range(ring):
            at = (source + 1) * depth - TILE
            lists[source : source + 1, :] = listed_ref[at : at + 1, :].astype(I32) - offset
        copy = pltpu.make_async_copy(lists, wanted, list_sem)
        copy.start()
        for side, ref in ((1, own_ref), (2 - 2 * odd, near_ref), (2 * odd, far_ref)):
            for block in range(blocks):
                at = side * blocks + block
                table[at] = ref[0:members, block * LANES : (block + 1) * LANES]
                innov_table[at] = ref[members : members + 1, block * LANES : (block + 1) * LANES]
        copy.wait()

        def compact(patch, order):
            count = jnp.int32(0)
            places = [jnp.int32(0)] * FIXED
            for slot in range(slots):
                block = wanted[patch, slot]
                rest[order, count] = block
                if order:
                    rest[2, count] = jnp.int32(slot)
                    places = [jnp.where(block == f, slot, at) for f, at in zip(fixed, places)]
                found = [block == f for f in fixed]
                count = count + jnp.where(found[0] | found[1], 0, 1)
            return places

        copies = []
        for patch in range(ring):
            compact(patch, 0)
            for slot in range(others):
                staged[patch * members : (patch + 1) * members, slot * LANES : (slot + 1) * LANES] = table[rest[0, slot]]
            span = pl.ds(patch * members, members)
            copies.append(pltpu.make_async_copy(staged.at[span], out_ref.at[span], sems.at[patch]))
            copies[-1].start()
        places = compact(lax.axis_index("ring"), 1)
        for slot in range(others):
            scales_ref[slot : slot + 1, :] = innov_table[rest[1, slot]]
            scales_ref[slots + slot : slots + slot + 1, :] = weights_ref[pl.ds(rest[2, slot], 1), :]
        for which in range(FIXED):
            slot = others + which
            scales_ref[slot : slot + 1, :] = innov_table[fixed[which]]
            scales_ref[slots + slot : slots + slot + 1, :] = weights_ref[pl.ds(places[which], 1), :]
        for copy in copies:
            copy.wait()

    return pl.pallas_call(
        kernel,
        out_shape=(
            jax.ShapeDtypeStruct((ring * members, others * LANES), F32),
            pltpu.VMEM((2 * slots, LANES), F32),
        ),
        in_specs=whole(5),
        out_specs=(pl.BlockSpec(memory_space=pl.ANY), pl.BlockSpec(memory_space=pltpu.VMEM)),
        scratch_shapes=[
            pltpu.VMEM((3 * blocks, members, LANES), F32),
            pltpu.VMEM((3 * blocks, 1, LANES), F32),
            pltpu.VMEM((ring, LANES), I32),
            pltpu.VMEM((ring * members, others * LANES), F32),
            pltpu.SMEM((ring, LANES), I32),
            pltpu.SMEM((3, slots), I32),
            pltpu.SemaphoreType.DMA,
            pltpu.SemaphoreType.DMA((ring,)),
        ],
        name="select",
    )(*near(listed, weights, own, near_side, far_side))


def parts(value):
    high = value.astype(BF16)
    return high, (value - high.astype(F32)).astype(BF16)


def product(first, second):
    high1, low1 = first
    high2, low2 = second
    dot = lambda a, b: jnp.dot(a, b, preferred_element_type=F32)
    return dot(high1, high2) + (dot(high1, low2) + dot(low1, high2))


def analyse(obs, scales, packed, crossed, rows):
    members, _ = obs.shape
    slots = scales.shape[0] // 2
    others = slots - FIXED
    groups = members // rows
    ring = groups // HALVES
    depth = packed.shape[0] // ring
    strips = crossed.shape[0] // (ring * rows)
    pieces = strips - FIXED
    width = pieces * LANES

    def kernel(obs_ref, scales_ref, packed_ref, crossed_ref, out_ref, columns):
        half = lax.axis_index("half")
        for source in range(ring):
            for strip in range(strips):
                lanes = slice(strip * LANES, (strip + 1) * LANES)
                skip = strip if strip < pieces else strip + pieces
                own = source * depth + skip * rows
                other = (source * strips + strip) * rows
                at = HALVES * source * rows
                columns[at : at + rows, lanes] = packed_ref[own : own + rows, :]
                columns[at + rows : at + HALVES * rows, lanes] = crossed_ref[other : other + rows, :]
        root_weights = jnp.sqrt(scales_ref[slots : 2 * slots, :])
        drive = jnp.zeros((members, LANES), F32)
        contract = lambda a, b: lax.dot_general(
            a, b, (((1,), (1,)), ((), ())), preferred_element_type=F32
        )
        highs, lows = [], []
        for slot in range(slots):
            if slot < others:
                block = obs_ref[:, slot * LANES : (slot + 1) * LANES]
            else:
                block = columns[:, width + (slot - others) * LANES : width + (slot - others + 1) * LANES]
            scaled = block * root_weights[slot : slot + 1, :]
            drive += scaled * (root_weights[slot : slot + 1, :] * scales_ref[slot : slot + 1, :])
            high, low = parts(scaled)
            highs.append(high)
            lows.append(low)
        high = jnp.concatenate(highs, axis=1)
        gram_matrix = contract(high, high)
        cross = contract(high, jnp.concatenate(lows, axis=1))
        gram_matrix += cross + cross.T
        drive = jnp.sum(drive, axis=1, keepdims=True)
        identity = (
            lax.broadcasted_iota(I32, (members, members), 0) == lax.broadcasted_iota(I32, (members, members), 1)
        ).astype(F32)
        system = identity + gram_matrix / (members - 1.0)
        trace_sum = jnp.sum(system * identity, keepdims=True)
        iterate_y = system / trace_sum
        half_three = 1.5 * identity
        factor = half_three - 0.5 * iterate_y
        y_parts = parts(iterate_y)
        z_parts = parts(factor)
        y_parts = parts(product(y_parts, z_parts))
        for repeat in range(1, NEWTON):
            factor = parts(half_three - 0.5 * product(z_parts, y_parts))
            iterate_z = product(factor, z_parts)
            if repeat < NEWTON - 1:
                y_parts = parts(product(y_parts, factor))
                z_parts = parts(iterate_z)
        root = iterate_z / jnp.sqrt(trace_sum)
        half_step = jnp.sum(root * drive, axis=0, keepdims=True)
        mean_weights = jnp.sum(root * half_step, axis=1, keepdims=True) / (members - 1.0)
        ens = columns[:, 0:width]
        ens_mean = jnp.mean(ens, axis=0, keepdims=True)
        anomalies = ens - ens_mean
        shift = ens_mean + jnp.sum(mean_weights * anomalies, axis=0, keepdims=True)
        updated = product(parts(root), parts(anomalies)) + shift
        for chunk in range(groups):
            group = (half ^ (chunk % HALVES)) * ring + chunk // HALVES
            at = pl.multiple_of(group * rows, TILE)
            out_ref[pl.ds(at, rows), :] = updated[chunk * rows : (chunk + 1) * rows, :]

    return pl.pallas_call(
        kernel,
        out_shape=pltpu.VMEM((members, width), F32),
        in_specs=whole(4),
        out_specs=pl.BlockSpec(memory_space=pltpu.VMEM),
        scratch_shapes=[pltpu.VMEM((members, strips * LANES), F32)],
        name="analyse",
    )(*near(obs, scales, packed, crossed))


def on_device(ensemble, obs_pert, innovation, block_list, loc_weights):
    regions = lax.axis_size("reg")
    rows, own_obs = obs_pert.shape
    weights = loc_weights.reshape(loc_weights.shape[1:])

    partner = lax.ppermute(obs_pert, "half", [(0, 1), (1, 0)])
    packed = pack(ensemble, obs_pert, block_list)
    packed = lax.all_to_all(packed, "ring", split_axis=0, concat_axis=0, tiled=True)
    table = jnp.concatenate([obs_pert, partner, innovation.reshape(1, own_obs)], axis=0)
    swaps = [[(i + a, i + 1 - a) for i in range(first, regions - 1, 2) for a in (0, 1)] for first in (0, 1)]
    far_side = lax.ppermute(table, "reg", swaps[1])
    near_side = lax.ppermute(table, "reg", swaps[0])
    chosen, scales = select(packed, block_list.shape[1], weights, table, near_side, far_side)
    obs = lax.all_to_all(chosen, "ring", split_axis=0, concat_axis=0, tiled=True)
    ring = lax.axis_size("ring")
    chunks = packed.reshape(ring, -1, LANES)
    part = ensemble.shape[1] // (HALVES * ring) // LANES * rows
    crossed = lax.ppermute(chunks[:, part : chunks.shape[1] - TILE, :].reshape(-1, LANES), "half", [(0, 1), (1, 0)])
    updated = analyse(obs, scales, packed, crossed, rows)
    sent = lax.all_to_all(updated, MEM, split_axis=0, concat_axis=0, tiled=True)
    return sent.reshape(sent.shape[0] // rows, rows, -1).transpose(1, 0, 2).reshape(rows, -1)


def solution(mesh):
    groups, regions = (mesh.shape[name] for name in ("mem", "reg"))
    fine = Mesh(mesh.devices.reshape(HALVES, groups // HALVES, regions), MEM + ("reg",))
    return jax.shard_map(
        on_device,
        mesh=fine,
        in_specs=(
            P(MEM, "reg"),
            P(MEM, "reg"),
            P("reg"),
            P(("reg",) + MEM, None),
            P(("reg",) + MEM, None, None),
        ),
        out_specs=P(MEM, "reg"),
        check_vma=False,
    )
```

```python
import jax
import jax.numpy as jnp
from jax import lax
from jax.experimental import pallas as pl
from jax.experimental.pallas import tpu as pltpu
from jax.sharding import Mesh
from jax.sharding import PartitionSpec as P


NEWTON = 8
LANES = 128
TILE = 8
HALVES = 2
FIXED = 2
F32 = jnp.float32
BF16 = jnp.bfloat16
I32 = jnp.int32
MEM = ("half", "ring")


def whole(count):
    return [pl.BlockSpec(memory_space=pltpu.VMEM)] * count


def near(*arrays):
    return [pltpu.with_memory_space_constraint(value, pltpu.VMEM) for value in arrays]


def pack(ensemble, obs_pert, block_list):
    rows, columns = ensemble.shape
    obs = obs_pert.shape[1]
    slots = block_list.shape[1]
    ring = lax.axis_size("ring")
    width = columns // (HALVES * ring)
    pieces = width // LANES
    depth = (HALVES * pieces + FIXED) * rows + TILE

    def kernel(ens_ref, obs_ref, list_ref, out_ref):
        half = lax.axis_index("half")
        for target in range(ring):
            at = target * depth
            for other in range(HALVES):
                patch = (half ^ other) * ring + target
                for piece in range(pieces):
                    start = pl.multiple_of(patch * width + piece * LANES, LANES)
                    out_ref[at : at + rows, :] = ens_ref[:, pl.ds(start, LANES)]
                    at += rows
            for start in (0, obs - LANES):
                out_ref[at : at + rows, :] = obs_ref[:, start : start + LANES]
                at += rows
            out_ref[at : at + TILE, :] = jnp.zeros((TILE, LANES), F32)
            out_ref[at : at + 1, 0:slots] = list_ref[...].astype(F32)

    return pl.pallas_call(
        kernel,
        out_shape=pltpu.VMEM((ring * depth, LANES), F32),
        in_specs=whole(3),
        out_specs=pl.BlockSpec(memory_space=pltpu.VMEM),
        name="pack",
    )(ensemble, obs_pert, block_list)


def select(listed, slots, weights, own, near_side, far_side):
    members = own.shape[0] - 1
    blocks = own.shape[1] // LANES
    others = slots - FIXED
    ring = lax.axis_size("ring")
    depth = listed.shape[0] // ring
    fixed = (blocks, 2 * blocks - 1)

    def kernel(
        listed_ref, weights_ref, own_ref, near_ref, far_ref, out_ref, scales_ref,
        table, innov_table, lists, staged, wanted, rest, list_sem, sems,
    ):
        region = lax.axis_index("reg")
        offset = (region - 1) * blocks
        odd = lax.rem(region, 2)
        for source in range(ring):
            at = (source + 1) * depth - TILE
            lists[source : source + 1, :] = listed_ref[at : at + 1, :].astype(I32) - offset
        copy = pltpu.make_async_copy(lists, wanted, list_sem)
        copy.start()
        for side, ref in ((1, own_ref), (2 - 2 * odd, near_ref), (2 * odd, far_ref)):
            for block in range(blocks):
                at = side * blocks + block
                table[at] = ref[0:members, block * LANES : (block + 1) * LANES]
                innov_table[at] = ref[members : members + 1, block * LANES : (block + 1) * LANES]
        copy.wait()

        def compact(patch, order):
            count = jnp.int32(0)
            places = [jnp.int32(0)] * FIXED
            for slot in range(slots):
                block = wanted[patch, slot]
                rest[order, count] = block
                if order:
                    rest[2, count] = jnp.int32(slot)
                    places = [jnp.where(block == f, slot, at) for f, at in zip(fixed, places)]
                found = [block == f for f in fixed]
                count = count + jnp.where(found[0] | found[1], 0, 1)
            return places

        copies = []
        for patch in range(ring):
            compact(patch, 0)
            for slot in range(others):
                staged[patch * members : (patch + 1) * members, slot * LANES : (slot + 1) * LANES] = table[rest[0, slot]]
            span = pl.ds(patch * members, members)
            copies.append(pltpu.make_async_copy(staged.at[span], out_ref.at[span], sems.at[patch]))
            copies[-1].start()
        places = compact(lax.axis_index("ring"), 1)
        for slot in range(others):
            scales_ref[slot : slot + 1, :] = innov_table[rest[1, slot]]
            scales_ref[slots + slot : slots + slot + 1, :] = weights_ref[pl.ds(rest[2, slot], 1), :]
        for which in range(FIXED):
            slot = others + which
            scales_ref[slot : slot + 1, :] = innov_table[fixed[which]]
            scales_ref[slots + slot : slots + slot + 1, :] = weights_ref[pl.ds(places[which], 1), :]
        for copy in copies:
            copy.wait()

    return pl.pallas_call(
        kernel,
        out_shape=(
            jax.ShapeDtypeStruct((ring * members, others * LANES), F32),
            pltpu.VMEM((2 * slots, LANES), F32),
        ),
        in_specs=whole(5),
        out_specs=(pl.BlockSpec(memory_space=pl.ANY), pl.BlockSpec(memory_space=pltpu.VMEM)),
        scratch_shapes=[
            pltpu.VMEM((3 * blocks, members, LANES), F32),
            pltpu.VMEM((3 * blocks, 1, LANES), F32),
            pltpu.VMEM((ring, LANES), I32),
            pltpu.VMEM((ring * members, others * LANES), F32),
            pltpu.SMEM((ring, LANES), I32),
            pltpu.SMEM((3, slots), I32),
            pltpu.SemaphoreType.DMA,
            pltpu.SemaphoreType.DMA((ring,)),
        ],
        name="select",
    )(*near(listed, weights, own, near_side, far_side))


def parts(value):
    high = value.astype(BF16)
    return high, (value - high.astype(F32)).astype(BF16)


def product(first, second):
    high1, low1 = first
    high2, low2 = second
    dot = lambda a, b: jnp.dot(a, b, preferred_element_type=F32)
    return dot(high1, high2) + (dot(high1, low2) + dot(low1, high2))


def analyse(obs, scales, packed, crossed, rows):
    members, _ = obs.shape
    slots = scales.shape[0] // 2
    others = slots - FIXED
    groups = members // rows
    ring = groups // HALVES
    depth = packed.shape[0] // ring
    strips = crossed.shape[0] // (ring * rows)
    pieces = strips - FIXED
    width = pieces * LANES

    def kernel(obs_ref, scales_ref, packed_ref, crossed_ref, out_ref, columns):
        half = lax.axis_index("half")
        for source in range(ring):
            for strip in range(strips):
                lanes = slice(strip * LANES, (strip + 1) * LANES)
                skip = strip if strip < pieces else strip + pieces
                own = source * depth + skip * rows
                other = (source * strips + strip) * rows
                at = HALVES * source * rows
                columns[at : at + rows, lanes] = packed_ref[own : own + rows, :]
                columns[at + rows : at + HALVES * rows, lanes] = crossed_ref[other : other + rows, :]
        root_weights = jnp.sqrt(scales_ref[slots : 2 * slots, :])
        drive = jnp.zeros((members, LANES), F32)
        contract = lambda a, b: lax.dot_general(
            a, b, (((1,), (1,)), ((), ())), preferred_element_type=F32
        )
        highs, lows = [], []
        for slot in range(slots):
            if slot < others:
                block = obs_ref[:, slot * LANES : (slot + 1) * LANES]
            else:
                block = columns[:, width + (slot - others) * LANES : width + (slot - others + 1) * LANES]
            scaled = block * root_weights[slot : slot + 1, :]
            drive += scaled * (root_weights[slot : slot + 1, :] * scales_ref[slot : slot + 1, :])
            high, low = parts(scaled)
            highs.append(high)
            lows.append(low)
        high = jnp.concatenate(highs, axis=1)
        gram_matrix = contract(high, high)
        cross = contract(high, jnp.concatenate(lows, axis=1))
        gram_matrix += cross + cross.T
        drive = jnp.sum(drive, axis=1, keepdims=True)
        identity = (
            lax.broadcasted_iota(I32, (members, members), 0) == lax.broadcasted_iota(I32, (members, members), 1)
        ).astype(F32)
        system = identity + gram_matrix / (members - 1.0)
        trace_sum = jnp.sum(system * identity, keepdims=True)
        iterate_y = system / trace_sum
        half_three = 1.5 * identity
        factor = half_three - 0.5 * iterate_y
        y_parts = parts(iterate_y)
        z_parts = parts(factor)
        y_parts = parts(product(y_parts, z_parts))
        for repeat in range(1, NEWTON):
            factor = parts(half_three - 0.5 * product(z_parts, y_parts))
            iterate_z = product(factor, z_parts)
            if repeat < NEWTON - 1:
                y_parts = parts(product(y_parts, factor))
                z_parts = parts(iterate_z)
        root = iterate_z / jnp.sqrt(trace_sum)
        half_step = jnp.sum(root * drive, axis=0, keepdims=True)
        mean_weights = jnp.sum(root * half_step, axis=1, keepdims=True) / (members - 1.0)
        ens = columns[:, 0:width]
        ens_mean = jnp.mean(ens, axis=0, keepdims=True)
        anomalies = ens - ens_mean
        shift = ens_mean + jnp.sum(mean_weights * anomalies, axis=0, keepdims=True)
        updated = product(parts(root), parts(anomalies)) + shift
        for chunk in range(groups):
            group = (half ^ (chunk % HALVES)) * ring + chunk // HALVES
            at = pl.multiple_of(group * rows, TILE)
            out_ref[pl.ds(at, rows), :] = updated[chunk * rows : (chunk + 1) * rows, :]

    return pl.pallas_call(
        kernel,
        out_shape=pltpu.VMEM((members, width), F32),
        in_specs=whole(4),
        out_specs=pl.BlockSpec(memory_space=pltpu.VMEM),
        scratch_shapes=[pltpu.VMEM((members, strips * LANES), F32)],
        name="analyse",
    )(*near(obs, scales, packed, crossed))


def on_device(ensemble, obs_pert, innovation, block_list, loc_weights):
    regions = lax.axis_size("reg")
    rows, own_obs = obs_pert.shape
    weights = loc_weights.reshape(loc_weights.shape[1:])

    partner = lax.ppermute(obs_pert, "half", [(0, 1), (1, 0)])
    packed = pack(ensemble, obs_pert, block_list)
    packed = lax.all_to_all(packed, "ring", split_axis=0, concat_axis=0, tiled=True)
    table = jnp.concatenate([obs_pert, partner, innovation.reshape(1, own_obs)], axis=0)
    swaps = [[(i + a, i + 1 - a) for i in range(first, regions - 1, 2) for a in (0, 1)] for first in (0, 1)]
    far_side = lax.ppermute(table, "reg", swaps[1])
    near_side = lax.ppermute(table, "reg", swaps[0])
    chosen, scales = select(packed, block_list.shape[1], weights, table, near_side, far_side)
    obs = lax.all_to_all(chosen, "ring", split_axis=0, concat_axis=0, tiled=True)
    ring = lax.axis_size("ring")
    chunks = packed.reshape(ring, -1, LANES)
    part = ensemble.shape[1] // (HALVES * ring) // LANES * rows
    crossed = lax.ppermute(chunks[:, part : chunks.shape[1] - TILE, :].reshape(-1, LANES), "half", [(0, 1), (1, 0)])
    updated = analyse(obs, scales, packed, crossed, rows)
    sent = lax.all_to_all(updated, MEM, split_axis=0, concat_axis=0, tiled=True)
    return sent.reshape(sent.shape[0] // rows, rows, -1).transpose(1, 0, 2).reshape(rows, -1)


def solution(mesh):
    groups, regions = (mesh.shape[name] for name in ("mem", "reg"))
    fine = Mesh(mesh.devices.reshape(HALVES, groups // HALVES, regions), MEM + ("reg",))
    return jax.shard_map(
        on_device,
        mesh=fine,
        in_specs=(
            P(MEM, "reg"),
            P(MEM, "reg"),
            P("reg"),
            P(("reg",) + MEM, None),
            P(("reg",) + MEM, None, None),
        ),
        out_specs=P(MEM, "reg"),
        check_vma=False,
    )
```

```python
import jax
import jax.numpy as jnp
from jax import lax
from jax.experimental import pallas as pl
from jax.experimental.pallas import tpu as pltpu
from jax.sharding import Mesh
from jax.sharding import PartitionSpec as P


NEWTON = 8
LANES = 128
TILE = 8
HALVES = 2
FIXED = 2
F32 = jnp.float32
BF16 = jnp.bfloat16
I32 = jnp.int32
MEM = ("half", "ring")


def whole(count):
    return [pl.BlockSpec(memory_space=pltpu.VMEM)] * count


def near(*arrays):
    return [pltpu.with_memory_space_constraint(value, pltpu.VMEM) for value in arrays]


def pack(ensemble, obs_pert, block_list):
    rows, columns = ensemble.shape
    obs = obs_pert.shape[1]
    slots = block_list.shape[1]
    ring = lax.axis_size("ring")
    width = columns // (HALVES * ring)
    pieces = width // LANES
    depth = (HALVES * pieces + FIXED) * rows + TILE

    side = ring * width
    batch = 2

    def kernel(ens_ref, obs_ref, list_ref, out_ref, ens_in, fixed_in, listed, tile, staged, in_sems, out_sems):
        half = lax.axis_index("half")

        def fetch(source, target, at):
            copy = pltpu.make_async_copy(source, target, in_sems.at[at])
            copy.start()
            return copy

        fetches = []
        for first in range(0, ring, batch):
            lanes = slice(first * width, (first + batch) * width)
            for other in range(HALVES):
                start = pl.multiple_of((half ^ other) * side + first * width, LANES)
                source = ens_ref.at[:, pl.ds(start, batch * width)]
                fetches.append(fetch(source, ens_in.at[other, :, lanes], len(fetches)))
        small = [fetch(list_ref, listed, len(fetches))]
        for which, start in enumerate((0, obs - LANES)):
            small.append(fetch(obs_ref.at[:, start : start + LANES], fixed_in.at[which], len(fetches) + 1 + which))
        tile[...] = jnp.zeros_like(tile)
        for copy in small:
            copy.wait()
        tile[0:1, 0:slots] = listed[...].astype(F32)
        last = tile[...]
        fixed = [fixed_in[which] for which in range(FIXED)]
        sends = []
        for target in range(ring):
            if target % batch == 0:
                for copy in fetches[target // batch * HALVES : (target // batch + 1) * HALVES]:
                    copy.wait()
            at = target * depth
            for other in range(HALVES):
                for piece in range(pieces):
                    start = target * width + piece * LANES
                    staged[at : at + rows, :] = ens_in[other, :, start : start + LANES]
                    at += rows
            for block in fixed:
                staged[at : at + rows, :] = block
                at += rows
            staged[at : at + TILE, :] = last
            span = pl.ds(target * depth, depth)
            sends.append(pltpu.make_async_copy(staged.at[span], out_ref.at[span], out_sems.at[target]))
            sends[-1].start()
        for copy in sends:
            copy.wait()

    return pl.pallas_call(
        kernel,
        out_shape=jax.ShapeDtypeStruct((ring * depth, LANES), F32),
        in_specs=[pl.BlockSpec(memory_space=pl.ANY)] * 3,
        out_specs=pl.BlockSpec(memory_space=pl.ANY),
        scratch_shapes=[
            pltpu.VMEM((HALVES, rows, side), F32),
            pltpu.VMEM((FIXED, rows, LANES), F32),
            pltpu.VMEM((1, slots), I32),
            pltpu.VMEM((TILE, LANES), F32),
            pltpu.VMEM((ring * depth, LANES), F32),
            pltpu.SemaphoreType.DMA((ring // batch * HALVES + 1 + FIXED,)),
            pltpu.SemaphoreType.DMA((ring,)),
        ],
        name="pack",
    )(ensemble, obs_pert, block_list)


def select(listed, slots, weights, own, near_side, far_side):
    members = own.shape[0] - 1
    blocks = own.shape[1] // LANES
    others = slots - FIXED
    ring = lax.axis_size("ring")
    depth = listed.shape[0] // ring
    fixed = (blocks, 2 * blocks - 1)

    def kernel(
        listed_ref, weights_ref, own_ref, near_ref, far_ref, out_ref, scales_ref,
        table, innov_table, lists, staged, wanted, rest, list_sem, sems,
    ):
        region = lax.axis_index("reg")
        offset = (region - 1) * blocks
        odd = lax.rem(region, 2)
        for source in range(ring):
            at = (source + 1) * depth - TILE
            lists[source : source + 1, :] = listed_ref[at : at + 1, :].astype(I32) - offset
        copy = pltpu.make_async_copy(lists, wanted, list_sem)
        copy.start()
        for side, ref in ((1, own_ref), (2 - 2 * odd, near_ref), (2 * odd, far_ref)):
            for block in range(blocks):
                at = side * blocks + block
                table[at] = ref[0:members, block * LANES : (block + 1) * LANES]
                innov_table[at] = ref[members : members + 1, block * LANES : (block + 1) * LANES]
        copy.wait()

        def compact(patch, order):
            count = jnp.int32(0)
            places = [jnp.int32(0)] * FIXED
            for slot in range(slots):
                block = wanted[patch, slot]
                rest[order, count] = block
                if order:
                    rest[2, count] = jnp.int32(slot)
                    places = [jnp.where(block == f, slot, at) for f, at in zip(fixed, places)]
                found = [block == f for f in fixed]
                count = count + jnp.where(found[0] | found[1], 0, 1)
            return places

        copies = []
        for patch in range(ring):
            compact(patch, 0)
            for slot in range(others):
                staged[patch * members : (patch + 1) * members, slot * LANES : (slot + 1) * LANES] = table[rest[0, slot]]
            span = pl.ds(patch * members, members)
            copies.append(pltpu.make_async_copy(staged.at[span], out_ref.at[span], sems.at[patch]))
            copies[-1].start()
        places = compact(lax.axis_index("ring"), 1)
        for slot in range(others):
            scales_ref[slot : slot + 1, :] = innov_table[rest[1, slot]]
            scales_ref[slots + slot : slots + slot + 1, :] = weights_ref[pl.ds(rest[2, slot], 1), :]
        for which in range(FIXED):
            slot = others + which
            scales_ref[slot : slot + 1, :] = innov_table[fixed[which]]
            scales_ref[slots + slot : slots + slot + 1, :] = weights_ref[pl.ds(places[which], 1), :]
        for copy in copies:
            copy.wait()

    return pl.pallas_call(
        kernel,
        out_shape=(
            jax.ShapeDtypeStruct((ring * members, others * LANES), F32),
            pltpu.VMEM((2 * slots, LANES), F32),
        ),
        in_specs=whole(5),
        out_specs=(pl.BlockSpec(memory_space=pl.ANY), pl.BlockSpec(memory_space=pltpu.VMEM)),
        scratch_shapes=[
            pltpu.VMEM((3 * blocks, members, LANES), F32),
            pltpu.VMEM((3 * blocks, 1, LANES), F32),
            pltpu.VMEM((ring, LANES), I32),
            pltpu.VMEM((ring * members, others * LANES), F32),
            pltpu.SMEM((ring, LANES), I32),
            pltpu.SMEM((3, slots), I32),
            pltpu.SemaphoreType.DMA,
            pltpu.SemaphoreType.DMA((ring,)),
        ],
        name="select",
    )(*near(listed, weights, own, near_side, far_side))


def parts(value):
    high = value.astype(BF16)
    return high, (value - high.astype(F32)).astype(BF16)


def product(first, second):
    high1, low1 = first
    high2, low2 = second
    dot = lambda a, b: jnp.dot(a, b, preferred_element_type=F32)
    rows = high1.shape[0] // 2
    done = []
    for at in range(0, high1.shape[0], rows):
        low, high = low1[at : at + rows], high1[at : at + rows]
        both = dot(jnp.concatenate([low, high], axis=0), high2)
        done.append(both[rows:] + (both[0:rows] + dot(high, low2)))
    return jnp.concatenate(done, axis=0)


def scale(block, scales, slot, slots):
    roots = jnp.sqrt(scales[slots + slot : slots + slot + 1, :])
    scaled = block * roots
    return parts(scaled), scaled * (roots * scales[slot : slot + 1, :])


def contract(first, second):
    return lax.dot_general(first, second, (((1,), (1,)), ((), ())), preferred_element_type=F32)


def gram(pieces):
    high, low = (jnp.concatenate(piece, axis=1) for piece in zip(*pieces))
    cross = contract(high, low)
    return contract(high, high) + (cross + cross.T)


def prepare(scales, packed, crossed, rows):
    slots = scales.shape[0] // 2
    ring = lax.axis_size("ring")
    members = HALVES * ring * rows
    depth = packed.shape[0] // ring
    strips = crossed.shape[0] // (ring * rows)
    pieces = strips - FIXED
    width = pieces * LANES

    def kernel(scales_ref, packed_ref, crossed_ref, high_ref, low_ref, mean_ref, gram_ref, drive_ref, columns):
        for source in range(ring):
            for strip in range(strips):
                lanes = slice(strip * LANES, (strip + 1) * LANES)
                skip = strip if strip < pieces else strip + pieces
                own = source * depth + skip * rows
                other = (source * strips + strip) * rows
                at = HALVES * source * rows
                columns[at : at + rows, lanes] = packed_ref[own : own + rows, :]
                columns[at + rows : at + HALVES * rows, lanes] = crossed_ref[other : other + rows, :]
        scales = scales_ref[...]
        made = [
            scale(columns[:, width + which * LANES : width + (which + 1) * LANES], scales, slots - FIXED + which, slots)
            for which in range(FIXED)
        ]
        gram_ref[...] = gram([piece for piece, share in made])
        drive_ref[...] = sum(share for piece, share in made)
        ens = columns[:, 0:width]
        ens_mean = jnp.mean(ens, axis=0, keepdims=True)
        high_ref[...], low_ref[...] = parts(ens - ens_mean)
        mean_ref[...] = jnp.broadcast_to(ens_mean, mean_ref.shape)

    return pl.pallas_call(
        kernel,
        out_shape=(
            pltpu.VMEM((members, width), BF16),
            pltpu.VMEM((members, width), BF16),
            pltpu.VMEM((TILE, width), F32),
            pltpu.VMEM((members, members), F32),
            pltpu.VMEM((members, LANES), F32),
        ),
        in_specs=whole(3),
        out_specs=tuple(whole(5)),
        scratch_shapes=[pltpu.VMEM((members, strips * LANES), F32)],
        name="prepare",
    )(*near(scales, packed, crossed))


def analyse(obs, scales, prepared, rows):
    members, _ = obs.shape
    slots = scales.shape[0] // 2
    groups = members // rows
    ring = groups // HALVES
    width = prepared[0].shape[1]

    def kernel(obs_ref, scales_ref, high_ref, low_ref, mean_ref, gram_ref, drive_ref, out_ref):
        half = lax.axis_index("half")
        scales = scales_ref[...]
        made = [
            scale(obs_ref[:, slot * LANES : (slot + 1) * LANES], scales, slot, slots) for slot in range(slots - FIXED)
        ]
        drive = drive_ref[...] + sum(share for piece, share in made)
        gram_matrix = gram_ref[...] + gram([piece for piece, share in made])
        drive = jnp.sum(drive, axis=1, keepdims=True)
        identity = (
            lax.broadcasted_iota(I32, (members, members), 0) == lax.broadcasted_iota(I32, (members, members), 1)
        ).astype(F32)
        system = identity + gram_matrix / (members - 1.0)
        trace_sum = jnp.sum(system * identity, keepdims=True)
        iterate_y = system / trace_sum
        half_three = 1.5 * identity
        factor = half_three - 0.5 * iterate_y
        y_parts = parts(iterate_y)
        z_parts = parts(factor)
        y_parts = parts(product(y_parts, z_parts))
        for repeat in range(1, NEWTON):
            factor = parts(half_three - 0.5 * product(z_parts, y_parts))
            iterate_z = product(factor, z_parts)
            if repeat < NEWTON - 1:
                y_parts = parts(product(y_parts, factor))
                z_parts = parts(iterate_z)
        root = iterate_z / jnp.sqrt(trace_sum)
        half_step = jnp.sum(root * drive, axis=0, keepdims=True)
        mean_weights = jnp.sum(root * half_step, axis=1, keepdims=True) / (members - 1.0)
        anomalies = (high_ref[...], low_ref[...])
        spread = anomalies[0].astype(F32) + anomalies[1].astype(F32)
        shift = mean_ref[0:1, :] + jnp.sum(mean_weights * spread, axis=0, keepdims=True)
        updated = product(parts(root), anomalies) + shift
        for chunk in range(groups):
            group = (half ^ (chunk % HALVES)) * ring + chunk // HALVES
            at = pl.multiple_of(group * rows, TILE)
            out_ref[pl.ds(at, rows), :] = updated[chunk * rows : (chunk + 1) * rows, :]

    return pl.pallas_call(
        kernel,
        out_shape=pltpu.VMEM((members, width), F32),
        in_specs=whole(7),
        out_specs=pl.BlockSpec(memory_space=pltpu.VMEM),
        name="analyse",
    )(*near(obs, scales, *prepared))


def on_device(ensemble, obs_pert, innovation, block_list, loc_weights):
    regions = lax.axis_size("reg")
    rows, own_obs = obs_pert.shape
    weights = loc_weights.reshape(loc_weights.shape[1:])

    partner = lax.ppermute(obs_pert, "half", [(0, 1), (1, 0)])
    packed = pack(ensemble, obs_pert, block_list)
    packed = lax.all_to_all(packed, "ring", split_axis=0, concat_axis=0, tiled=True)
    table = jnp.concatenate([obs_pert, partner, innovation.reshape(1, own_obs)], axis=0)
    swaps = [[(i + a, i + 1 - a) for i in range(first, regions - 1, 2) for a in (0, 1)] for first in (0, 1)]
    far_side = lax.ppermute(table, "reg", swaps[1])
    near_side = lax.ppermute(table, "reg", swaps[0])
    chosen, scales = select(packed, block_list.shape[1], weights, table, near_side, far_side)
    obs = lax.all_to_all(chosen, "ring", split_axis=0, concat_axis=0, tiled=True)
    ring = lax.axis_size("ring")
    chunks = packed.reshape(ring, -1, LANES)
    part = ensemble.shape[1] // (HALVES * ring) // LANES * rows
    crossed = lax.ppermute(chunks[:, part : chunks.shape[1] - TILE, :].reshape(-1, LANES), "half", [(0, 1), (1, 0)])
    prepared = prepare(scales, packed, crossed, rows)
    updated = analyse(obs, scales, prepared, rows)
    sent = lax.all_to_all(updated, MEM, split_axis=0, concat_axis=0, tiled=True)
    return sent.reshape(sent.shape[0] // rows, rows, -1).transpose(1, 0, 2).reshape(rows, -1)


def solution(mesh):
    groups, regions = (mesh.shape[name] for name in ("mem", "reg"))
    fine = Mesh(mesh.devices.reshape(HALVES, groups // HALVES, regions), MEM + ("reg",))
    return jax.shard_map(
        on_device,
        mesh=fine,
        in_specs=(
            P(MEM, "reg"),
            P(MEM, "reg"),
            P("reg"),
            P(("reg",) + MEM, None),
            P(("reg",) + MEM, None, None),
        ),
        out_specs=P(MEM, "reg"),
        check_vma=False,
    )
```

```python
import jax
import jax.numpy as jnp
from jax import lax
from jax.experimental import pallas as pl
from jax.experimental.pallas import tpu as pltpu
from jax.sharding import Mesh
from jax.sharding import PartitionSpec as P


NEWTON = 8
LANES = 128
TILE = 8
HALVES = 2
FIXED = 2
F32 = jnp.float32
BF16 = jnp.bfloat16
I32 = jnp.int32
MEM = ("half", "ring")


def whole(count):
    return [pl.BlockSpec(memory_space=pltpu.VMEM)] * count


def near(*arrays):
    return [pltpu.with_memory_space_constraint(value, pltpu.VMEM) for value in arrays]


def pack(ensemble, obs_pert, block_list):
    rows, columns = ensemble.shape
    obs = obs_pert.shape[1]
    slots = block_list.shape[1]
    ring = lax.axis_size("ring")
    width = columns // (HALVES * ring)
    pieces = width // LANES
    depth = (HALVES * pieces + FIXED) * rows + TILE

    def kernel(ens_ref, obs_ref, list_ref, out_ref):
        half = lax.axis_index("half")
        for target in range(ring):
            at = target * depth
            for other in range(HALVES):
                patch = (half ^ other) * ring + target
                for piece in range(pieces):
                    start = pl.multiple_of(patch * width + piece * LANES, LANES)
                    out_ref[at : at + rows, :] = ens_ref[:, pl.ds(start, LANES)]
                    at += rows
            for start in (0, obs - LANES):
                out_ref[at : at + rows, :] = obs_ref[:, start : start + LANES]
                at += rows
            out_ref[at : at + TILE, :] = jnp.zeros((TILE, LANES), F32)
            out_ref[at : at + 1, 0:slots] = list_ref[...].astype(F32)

    return pl.pallas_call(
        kernel,
        out_shape=pltpu.VMEM((ring * depth, LANES), F32),
        in_specs=whole(3),
        out_specs=pl.BlockSpec(memory_space=pltpu.VMEM),
        name="pack",
    )(ensemble, obs_pert, block_list)


def select(listed, slots, weights, own, near_side, far_side):
    members = own.shape[0] - 1
    blocks = own.shape[1] // LANES
    others = slots - FIXED
    ring = lax.axis_size("ring")
    depth = listed.shape[0] // ring
    fixed = (blocks, 2 * blocks - 1)

    def kernel(
        listed_ref, weights_ref, own_ref, near_ref, far_ref, out_ref, scales_ref,
        table, innov_table, lists, staged, wanted, rest, list_sem, sems,
    ):
        region = lax.axis_index("reg")
        offset = (region - 1) * blocks
        odd = lax.rem(region, 2)
        for source in range(ring):
            at = (source + 1) * depth - TILE
            lists[source : source + 1, :] = listed_ref[at : at + 1, :].astype(I32) - offset
        copy = pltpu.make_async_copy(lists, wanted, list_sem)
        copy.start()
        for side, ref in ((1, own_ref), (2 - 2 * odd, near_ref), (2 * odd, far_ref)):
            for block in range(blocks):
                at = side * blocks + block
                table[at] = ref[0:members, block * LANES : (block + 1) * LANES]
                innov_table[at] = ref[members : members + 1, block * LANES : (block + 1) * LANES]
        copy.wait()

        def compact(patch, order):
            count = jnp.int32(0)
            places = [jnp.int32(0)] * FIXED
            for slot in range(slots):
                block = wanted[patch, slot]
                rest[order, count] = block
                if order:
                    rest[2, count] = jnp.int32(slot)
                    places = [jnp.where(block == f, slot, at) for f, at in zip(fixed, places)]
                found = [block == f for f in fixed]
                count = count + jnp.where(found[0] | found[1], 0, 1)
            return places

        copies = []
        for patch in range(ring):
            compact(patch, 0)
            for slot in range(others):
                staged[patch * members : (patch + 1) * members, slot * LANES : (slot + 1) * LANES] = table[rest[0, slot]]
            span = pl.ds(patch * members, members)
            copies.append(pltpu.make_async_copy(staged.at[span], out_ref.at[span], sems.at[patch]))
            copies[-1].start()
        places = compact(lax.axis_index("ring"), 1)
        for slot in range(others):
            scales_ref[slot : slot + 1, :] = innov_table[rest[1, slot]]
            scales_ref[slots + slot : slots + slot + 1, :] = weights_ref[pl.ds(rest[2, slot], 1), :]
        for which in range(FIXED):
            slot = others + which
            scales_ref[slot : slot + 1, :] = innov_table[fixed[which]]
            scales_ref[slots + slot : slots + slot + 1, :] = weights_ref[pl.ds(places[which], 1), :]
        for copy in copies:
            copy.wait()

    return pl.pallas_call(
        kernel,
        out_shape=(
            jax.ShapeDtypeStruct((ring * members, others * LANES), F32),
            pltpu.VMEM((2 * slots, LANES), F32),
        ),
        in_specs=whole(5),
        out_specs=(pl.BlockSpec(memory_space=pl.ANY), pl.BlockSpec(memory_space=pltpu.VMEM)),
        scratch_shapes=[
            pltpu.VMEM((3 * blocks, members, LANES), F32),
            pltpu.VMEM((3 * blocks, 1, LANES), F32),
            pltpu.VMEM((ring, LANES), I32),
            pltpu.VMEM((ring * members, others * LANES), F32),
            pltpu.SMEM((ring, LANES), I32),
            pltpu.SMEM((3, slots), I32),
            pltpu.SemaphoreType.DMA,
            pltpu.SemaphoreType.DMA((ring,)),
        ],
        name="select",
    )(*near(listed, weights, own, near_side, far_side))


def parts(value):
    high = value.astype(BF16)
    return high, (value - high.astype(F32)).astype(BF16)


def product(first, second):
    high1, low1 = first
    high2, low2 = second
    dot = lambda a, b: jnp.dot(a, b, preferred_element_type=F32)
    rows = high1.shape[0] // 2
    done = []
    for at in range(0, high1.shape[0], rows):
        low, high = low1[at : at + rows], high1[at : at + rows]
        both = dot(jnp.concatenate([low, high], axis=0), high2)
        done.append(both[rows:] + (both[0:rows] + dot(high, low2)))
    return jnp.concatenate(done, axis=0)


def scale(block, scales, slot, slots):
    roots = jnp.sqrt(scales[slots + slot : slots + slot + 1, :])
    scaled = block * roots
    return parts(scaled), scaled * (roots * scales[slot : slot + 1, :])


def contract(first, second):
    return lax.dot_general(first, second, (((1,), (1,)), ((), ())), preferred_element_type=F32)


def gram(pieces):
    high, low = (jnp.concatenate(piece, axis=1) for piece in zip(*pieces))
    cross = contract(high, low)
    return contract(high, high) + (cross + cross.T)


def prepare(scales, packed, crossed, rows):
    slots = scales.shape[0] // 2
    ring = lax.axis_size("ring")
    members = HALVES * ring * rows
    depth = packed.shape[0] // ring
    strips = crossed.shape[0] // (ring * rows)
    pieces = strips - FIXED
    width = pieces * LANES

    def kernel(scales_ref, packed_ref, crossed_ref, high_ref, low_ref, mean_ref, gram_ref, drive_ref, columns):
        for source in range(ring):
            for strip in range(strips):
                lanes = slice(strip * LANES, (strip + 1) * LANES)
                skip = strip if strip < pieces else strip + pieces
                own = source * depth + skip * rows
                other = (source * strips + strip) * rows
                at = HALVES * source * rows
                columns[at : at + rows, lanes] = packed_ref[own : own + rows, :]
                columns[at + rows : at + HALVES * rows, lanes] = crossed_ref[other : other + rows, :]
        scales = scales_ref[...]
        made = [
            scale(columns[:, width + which * LANES : width + (which + 1) * LANES], scales, slots - FIXED + which, slots)
            for which in range(FIXED)
        ]
        gram_ref[...] = gram([piece for piece, share in made])
        drive_ref[...] = sum(share for piece, share in made)
        ens = columns[:, 0:width]
        ens_mean = jnp.mean(ens, axis=0, keepdims=True)
        high_ref[...], low_ref[...] = parts(ens - ens_mean)
        mean_ref[...] = jnp.broadcast_to(ens_mean, mean_ref.shape)

    return pl.pallas_call(
        kernel,
        out_shape=(
            pltpu.VMEM((members, width), BF16),
            pltpu.VMEM((members, width), BF16),
            pltpu.VMEM((TILE, width), F32),
            pltpu.VMEM((members, members), F32),
            pltpu.VMEM((members, LANES), F32),
        ),
        in_specs=whole(3),
        out_specs=tuple(whole(5)),
        scratch_shapes=[pltpu.VMEM((members, strips * LANES), F32)],
        name="prepare",
    )(*near(scales, packed, crossed))


def analyse(obs, scales, prepared, rows):
    members, _ = obs.shape
    slots = scales.shape[0] // 2
    groups = members // rows
    width = prepared[0].shape[1]

    def kernel(obs_ref, scales_ref, high_ref, low_ref, mean_ref, gram_ref, drive_ref, out_ref):
        half = lax.axis_index("half")
        scales = scales_ref[...]
        made = [
            scale(obs_ref[:, slot * LANES : (slot + 1) * LANES], scales, slot, slots) for slot in range(slots - FIXED)
        ]
        drive = drive_ref[...] + sum(share for piece, share in made)
        gram_matrix = gram_ref[...] + gram([piece for piece, share in made])
        drive = jnp.sum(drive, axis=1, keepdims=True)
        identity = (
            lax.broadcasted_iota(I32, (members, members), 0) == lax.broadcasted_iota(I32, (members, members), 1)
        ).astype(F32)
        system = identity + gram_matrix / (members - 1.0)
        trace_sum = jnp.sum(system * identity, keepdims=True)
        iterate_y = system / trace_sum
        half_three = 1.5 * identity
        factor = half_three - 0.5 * iterate_y
        y_parts = parts(iterate_y)
        z_parts = parts(factor)
        y_parts = parts(product(y_parts, z_parts))
        for repeat in range(1, NEWTON):
            factor = parts(half_three - 0.5 * product(z_parts, y_parts))
            if repeat < NEWTON - 1:
                iterate_y = product(y_parts, factor)
            iterate_z = product(factor, z_parts)
            if repeat < NEWTON - 1:
                y_parts = parts(iterate_y)
                z_parts = parts(iterate_z)
        root = iterate_z / jnp.sqrt(trace_sum)
        half_step = jnp.sum(root * drive, axis=0, keepdims=True)
        mean_weights = jnp.sum(root * half_step, axis=1, keepdims=True) / (members - 1.0)
        anomalies = (high_ref[...], low_ref[...])
        spread = anomalies[0].astype(F32) + anomalies[1].astype(F32)
        shift = mean_ref[0:1, :] + jnp.sum(mean_weights * spread, axis=0, keepdims=True)
        updated = product(parts(root), anomalies) + shift
        for chunk in range(groups):
            group = chunk // HALVES * HALVES + (half ^ (chunk % HALVES))
            at = pl.multiple_of(group * rows, TILE)
            out_ref[pl.ds(at, rows), :] = updated[chunk * rows : (chunk + 1) * rows, :]

    return pl.pallas_call(
        kernel,
        out_shape=pltpu.VMEM((members, width), F32),
        in_specs=whole(7),
        out_specs=pl.BlockSpec(memory_space=pltpu.VMEM),
        name="analyse",
    )(*near(obs, scales, *prepared))


def on_device(ensemble, obs_pert, innovation, block_list, loc_weights):
    regions = lax.axis_size("reg")
    rows, own_obs = obs_pert.shape
    weights = loc_weights.reshape(loc_weights.shape[1:])

    partner = lax.ppermute(obs_pert, "half", [(0, 1), (1, 0)])
    packed = pack(ensemble, obs_pert, block_list)
    packed = lax.all_to_all(packed, "ring", split_axis=0, concat_axis=0, tiled=True)
    table = jnp.concatenate([obs_pert, partner, innovation.reshape(1, own_obs)], axis=0)
    swaps = [[(i + a, i + 1 - a) for i in range(first, regions - 1, 2) for a in (0, 1)] for first in (0, 1)]
    far_side = lax.ppermute(table, "reg", swaps[1])
    near_side = lax.ppermute(table, "reg", swaps[0])
    chosen, scales = select(packed, block_list.shape[1], weights, table, near_side, far_side)
    obs = lax.all_to_all(chosen, "ring", split_axis=0, concat_axis=0, tiled=True)
    ring = lax.axis_size("ring")
    chunks = packed.reshape(ring, -1, LANES)
    part = ensemble.shape[1] // (HALVES * ring) // LANES * rows
    crossed = lax.ppermute(chunks[:, part : chunks.shape[1] - TILE, :].reshape(-1, LANES), "half", [(0, 1), (1, 0)])
    prepared = prepare(scales, packed, crossed, rows)
    updated = analyse(obs, scales, prepared, rows)
    sent = lax.all_to_all(updated, MEM[::-1], split_axis=0, concat_axis=0, tiled=True)
    sent = sent.reshape(ring, HALVES, rows // TILE, TILE, -1)
    return sent.transpose(2, 3, 1, 0, 4).reshape(rows, -1)


def solution(mesh):
    groups, regions = (mesh.shape[name] for name in ("mem", "reg"))
    fine = Mesh(mesh.devices.reshape(HALVES, groups // HALVES, regions), MEM + ("reg",))
    return jax.shard_map(
        on_device,
        mesh=fine,
        in_specs=(
            P(MEM, "reg"),
            P(MEM, "reg"),
            P("reg"),
            P(("reg",) + MEM, None),
            P(("reg",) + MEM, None, None),
        ),
        out_specs=P(MEM, "reg"),
        check_vma=False,
    )
```

```python
import jax
import jax.numpy as jnp
from jax import lax
from jax.experimental import pallas as pl
from jax.experimental.pallas import tpu as pltpu
from jax.sharding import Mesh
from jax.sharding import PartitionSpec as P


NEWTON = 8
LANES = 128
TILE = 8
HALVES = 2
FIXED = 2
F32 = jnp.float32
BF16 = jnp.bfloat16
I32 = jnp.int32
MEM = ("half", "ring")


def whole(count):
    return [pl.BlockSpec(memory_space=pltpu.VMEM)] * count


def near(*arrays):
    return [pltpu.with_memory_space_constraint(value, pltpu.VMEM) for value in arrays]


def pack(ensemble, obs_pert, block_list):
    rows, columns = ensemble.shape
    obs = obs_pert.shape[1]
    slots = block_list.shape[1]
    ring = lax.axis_size("ring")
    width = columns // (HALVES * ring)
    pieces = width // LANES
    depth = (HALVES * pieces + FIXED) * rows + TILE

    def kernel(ens_ref, obs_ref, list_ref, out_ref):
        half = lax.axis_index("half")
        for target in range(ring):
            at = target * depth
            for other in range(HALVES):
                patch = (half ^ other) * ring + target
                for piece in range(pieces):
                    start = pl.multiple_of(patch * width + piece * LANES, LANES)
                    out_ref[at : at + rows, :] = ens_ref[:, pl.ds(start, LANES)]
                    at += rows
            for start in (0, obs - LANES):
                out_ref[at : at + rows, :] = obs_ref[:, start : start + LANES]
                at += rows
            out_ref[at : at + TILE, :] = jnp.zeros((TILE, LANES), F32)
            out_ref[at : at + 1, 0:slots] = list_ref[...].astype(F32)

    return pl.pallas_call(
        kernel,
        out_shape=pltpu.VMEM((ring * depth, LANES), F32),
        in_specs=whole(3),
        out_specs=pl.BlockSpec(memory_space=pltpu.VMEM),
        name="pack",
    )(ensemble, obs_pert, block_list)


def select(listed, slots, weights, own, near_side, far_side):
    members = own.shape[0] - 1
    blocks = own.shape[1] // LANES
    others = slots - FIXED
    ring = lax.axis_size("ring")
    depth = listed.shape[0] // ring
    fixed = (blocks, 2 * blocks - 1)

    def kernel(
        listed_ref, weights_ref, own_ref, near_ref, far_ref, out_ref, scales_ref,
        table, innov_table, lists, staged, wanted, rest, list_sem, sems,
    ):
        region = lax.axis_index("reg")
        offset = (region - 1) * blocks
        odd = lax.rem(region, 2)
        for source in range(ring):
            at = (source + 1) * depth - TILE
            lists[source : source + 1, :] = listed_ref[at : at + 1, :].astype(I32) - offset
        copy = pltpu.make_async_copy(lists, wanted, list_sem)
        copy.start()
        for side, ref in ((1, own_ref), (2 - 2 * odd, near_ref), (2 * odd, far_ref)):
            for block in range(blocks):
                at = side * blocks + block
                table[at] = ref[0:members, block * LANES : (block + 1) * LANES]
                innov_table[at] = ref[members : members + 1, block * LANES : (block + 1) * LANES]
        copy.wait()

        def compact(patch, order):
            count = jnp.int32(0)
            places = [jnp.int32(0)] * FIXED
            for slot in range(slots):
                block = wanted[patch, slot]
                rest[order, count] = block
                if order:
                    rest[2, count] = jnp.int32(slot)
                    places = [jnp.where(block == f, slot, at) for f, at in zip(fixed, places)]
                found = [block == f for f in fixed]
                count = count + jnp.where(found[0] | found[1], 0, 1)
            return places

        copies = []
        for patch in range(ring):
            compact(patch, 0)
            for slot in range(others):
                staged[patch * members : (patch + 1) * members, slot * LANES : (slot + 1) * LANES] = table[rest[0, slot]]
            span = pl.ds(patch * members, members)
            copies.append(pltpu.make_async_copy(staged.at[span], out_ref.at[span], sems.at[patch]))
            copies[-1].start()
        places = compact(lax.axis_index("ring"), 1)
        for slot in range(others):
            scales_ref[slot : slot + 1, :] = innov_table[rest[1, slot]]
            scales_ref[slots + slot : slots + slot + 1, :] = weights_ref[pl.ds(rest[2, slot], 1), :]
        for which in range(FIXED):
            slot = others + which
            scales_ref[slot : slot + 1, :] = innov_table[fixed[which]]
            scales_ref[slots + slot : slots + slot + 1, :] = weights_ref[pl.ds(places[which], 1), :]
        for copy in copies:
            copy.wait()

    return pl.pallas_call(
        kernel,
        out_shape=(
            jax.ShapeDtypeStruct((ring * members, others * LANES), F32),
            pltpu.VMEM((2 * slots, LANES), F32),
        ),
        in_specs=whole(5),
        out_specs=(pl.BlockSpec(memory_space=pl.ANY), pl.BlockSpec(memory_space=pltpu.VMEM)),
        scratch_shapes=[
            pltpu.VMEM((3 * blocks, members, LANES), F32),
            pltpu.VMEM((3 * blocks, 1, LANES), F32),
            pltpu.VMEM((ring, LANES), I32),
            pltpu.VMEM((ring * members, others * LANES), F32),
            pltpu.SMEM((ring, LANES), I32),
            pltpu.SMEM((3, slots), I32),
            pltpu.SemaphoreType.DMA,
            pltpu.SemaphoreType.DMA((ring,)),
        ],
        name="select",
    )(*near(listed, weights, own, near_side, far_side))


def parts(value):
    high = value.astype(BF16)
    return high, (value - high.astype(F32)).astype(BF16)


def product(first, second):
    high1, low1 = first
    high2, low2 = second
    dot = lambda a, b: jnp.dot(a, b, preferred_element_type=F32)
    rows = high1.shape[0] // 2
    done = []
    for at in range(0, high1.shape[0], rows):
        low, high = low1[at : at + rows], high1[at : at + rows]
        both = dot(jnp.concatenate([low, high], axis=0), high2)
        done.append(both[rows:] + (both[0:rows] + dot(high, low2)))
    return jnp.concatenate(done, axis=0)


def scale(block, scales, slot, slots):
    roots = jnp.sqrt(scales[slots + slot : slots + slot + 1, :])
    scaled = block * roots
    return parts(scaled), scaled * (roots * scales[slot : slot + 1, :])


def contract(first, second):
    return lax.dot_general(first, second, (((1,), (1,)), ((), ())), preferred_element_type=F32)


def gram(pieces):
    high, low = (jnp.concatenate(piece, axis=1) for piece in zip(*pieces))
    cross = contract(high, low)
    return contract(high, high) + (cross + cross.T)


def prepare(scales, packed, crossed, rows):
    slots = scales.shape[0] // 2
    ring = lax.axis_size("ring")
    members = HALVES * ring * rows
    depth = packed.shape[0] // ring
    strips = crossed.shape[0] // (ring * rows)
    pieces = strips - FIXED
    width = pieces * LANES

    def kernel(scales_ref, packed_ref, crossed_ref, high_ref, low_ref, mean_ref, gram_ref, drive_ref, columns):
        for source in range(ring):
            for strip in range(strips):
                lanes = slice(strip * LANES, (strip + 1) * LANES)
                skip = strip if strip < pieces else strip + pieces
                own = source * depth + skip * rows
                other = (source * strips + strip) * rows
                at = HALVES * source * rows
                columns[at : at + rows, lanes] = packed_ref[own : own + rows, :]
                columns[at + rows : at + HALVES * rows, lanes] = crossed_ref[other : other + rows, :]
        scales = scales_ref[...]
        made = [
            scale(columns[:, width + which * LANES : width + (which + 1) * LANES], scales, slots - FIXED + which, slots)
            for which in range(FIXED)
        ]
        gram_ref[...] = gram([piece for piece, share in made])
        drive_ref[...] = sum(share for piece, share in made)
        ens = columns[:, 0:width]
        ens_mean = jnp.mean(ens, axis=0, keepdims=True)
        high_ref[...], low_ref[...] = parts(ens - ens_mean)
        mean_ref[...] = jnp.broadcast_to(ens_mean, mean_ref.shape)

    return pl.pallas_call(
        kernel,
        out_shape=(
            pltpu.VMEM((members, width), BF16),
            pltpu.VMEM((members, width), BF16),
            pltpu.VMEM((TILE, width), F32),
            pltpu.VMEM((members, members), F32),
            pltpu.VMEM((members, LANES), F32),
        ),
        in_specs=whole(3),
        out_specs=tuple(whole(5)),
        scratch_shapes=[pltpu.VMEM((members, strips * LANES), F32)],
        name="prepare",
    )(*near(scales, packed, crossed))


def analyse(obs, scales, prepared, rows):
    members, _ = obs.shape
    slots = scales.shape[0] // 2
    groups = members // rows
    ring = groups // HALVES
    width = prepared[0].shape[1]

    def kernel(obs_ref, scales_ref, high_ref, low_ref, mean_ref, gram_ref, drive_ref, out_ref):
        half = lax.axis_index("half")
        scales = scales_ref[...]
        made = [
            scale(obs_ref[:, slot * LANES : (slot + 1) * LANES], scales, slot, slots) for slot in range(slots - FIXED)
        ]
        drive = drive_ref[...] + sum(share for piece, share in made)
        gram_matrix = gram_ref[...] + gram([piece for piece, share in made])
        drive = jnp.sum(drive, axis=1, keepdims=True)
        identity = (
            lax.broadcasted_iota(I32, (members, members), 0) == lax.broadcasted_iota(I32, (members, members), 1)
        ).astype(F32)
        system = identity + gram_matrix / (members - 1.0)
        trace_sum = jnp.sum(system * identity, keepdims=True)
        iterate_y = system / trace_sum
        half_three = 1.5 * identity
        factor = half_three - 0.5 * iterate_y
        y_parts = parts(iterate_y)
        z_parts = parts(factor)
        y_parts = parts(product(y_parts, z_parts))
        for repeat in range(1, NEWTON):
            factor = parts(half_three - 0.5 * product(z_parts, y_parts))
            if repeat < NEWTON - 1:
                iterate_y = product(y_parts, factor)
            iterate_z = product(factor, z_parts)
            if repeat < NEWTON - 1:
                y_parts = parts(iterate_y)
                z_parts = parts(iterate_z)
        root = iterate_z / jnp.sqrt(trace_sum)
        half_step = jnp.sum(root * drive, axis=0, keepdims=True)
        mean_weights = jnp.sum(root * half_step, axis=1, keepdims=True) / (members - 1.0)
        anomalies = (high_ref[...], low_ref[...])
        spread = anomalies[0].astype(F32) + anomalies[1].astype(F32)
        shift = mean_ref[0:1, :] + jnp.sum(mean_weights * spread, axis=0, keepdims=True)
        updated = product(parts(root), anomalies) + shift
        for chunk in range(groups):
            group = (1 - (half ^ (chunk % HALVES))) * ring + chunk // HALVES
            at = pl.multiple_of(group * rows, TILE)
            out_ref[pl.ds(at, rows), :] = updated[chunk * rows : (chunk + 1) * rows, :]

    return pl.pallas_call(
        kernel,
        out_shape=pltpu.VMEM((members, width), F32),
        in_specs=whole(7),
        out_specs=pl.BlockSpec(memory_space=pltpu.VMEM),
        name="analyse",
    )(*near(obs, scales, *prepared))


def place(sent, order):
    groups = len(order)
    rows = sent.shape[0] // groups
    width = sent.shape[1]

    def kernel(sent_ref, out_ref, sems):
        copies = []
        for at, patch in enumerate(order):
            source = sent_ref.at[at * rows : (at + 1) * rows]
            target = out_ref.at[:, patch * width : (patch + 1) * width]
            copies.append(pltpu.make_async_copy(source, target, sems.at[at]))
            copies[-1].start()
        for copy in copies:
            copy.wait()

    return pl.pallas_call(
        kernel,
        out_shape=jax.ShapeDtypeStruct((rows, groups * width), F32),
        in_specs=whole(1),
        out_specs=pl.BlockSpec(memory_space=pl.ANY),
        scratch_shapes=[pltpu.SemaphoreType.DMA((groups,))],
        name="place",
    )(*near(sent))


def on_device(ensemble, obs_pert, innovation, block_list, loc_weights):
    regions = lax.axis_size("reg")
    rows, own_obs = obs_pert.shape
    weights = loc_weights.reshape(loc_weights.shape[1:])

    partner = lax.ppermute(obs_pert, "half", [(0, 1), (1, 0)])
    packed = pack(ensemble, obs_pert, block_list)
    packed = lax.all_to_all(packed, "ring", split_axis=0, concat_axis=0, tiled=True)
    table = jnp.concatenate([obs_pert, partner, innovation.reshape(1, own_obs)], axis=0)
    swaps = [[(i + a, i + 1 - a) for i in range(first, regions - 1, 2) for a in (0, 1)] for first in (0, 1)]
    far_side = lax.ppermute(table, "reg", swaps[1])
    near_side = lax.ppermute(table, "reg", swaps[0])
    chosen, scales = select(packed, block_list.shape[1], weights, table, near_side, far_side)
    obs = lax.all_to_all(chosen, "ring", split_axis=0, concat_axis=0, tiled=True)
    ring = lax.axis_size("ring")
    chunks = packed.reshape(ring, -1, LANES)
    part = ensemble.shape[1] // (HALVES * ring) // LANES * rows
    crossed = lax.ppermute(chunks[:, part : chunks.shape[1] - TILE, :].reshape(-1, LANES), "half", [(0, 1), (1, 0)])
    prepared = prepare(scales, packed, crossed, rows)
    updated = analyse(obs, scales, prepared, rows)
    order = [(i + ring) % (HALVES * ring) for i in range(HALVES * ring)]
    sent = lax.all_to_all(
        updated, MEM, split_axis=0, concat_axis=0, tiled=True, axis_index_groups=[order]
    )
    return place(sent, order)


def solution(mesh):
    groups, regions = (mesh.shape[name] for name in ("mem", "reg"))
    fine = Mesh(mesh.devices.reshape(HALVES, groups // HALVES, regions), MEM + ("reg",))
    return jax.shard_map(
        on_device,
        mesh=fine,
        in_specs=(
            P(MEM, "reg"),
            P(MEM, "reg"),
            P("reg"),
            P(("reg",) + MEM, None),
            P(("reg",) + MEM, None, None),
        ),
        out_specs=P(MEM, "reg"),
        check_vma=False,
    )
```

```python
import jax
import jax.numpy as jnp
from jax import lax
from jax.experimental import pallas as pl
from jax.experimental.pallas import tpu as pltpu
from jax.sharding import Mesh
from jax.sharding import PartitionSpec as P


NEWTON = 8
LANES = 128
TILE = 8
HALVES = 2
FIXED = 2
F32 = jnp.float32
BF16 = jnp.bfloat16
I32 = jnp.int32
MEM = ("half", "ring")


def whole(count):
    return [pl.BlockSpec(memory_space=pltpu.VMEM)] * count


def near(*arrays):
    return [pltpu.with_memory_space_constraint(value, pltpu.VMEM) for value in arrays]


def pack(ensemble, obs_pert, block_list):
    rows, columns = ensemble.shape
    obs = obs_pert.shape[1]
    slots = block_list.shape[1]
    ring = lax.axis_size("ring")
    width = columns // (HALVES * ring)
    pieces = width // LANES
    depth = (HALVES * pieces + FIXED) * rows + TILE

    def kernel(ens_ref, obs_ref, list_ref, out_ref):
        half = lax.axis_index("half")
        for target in range(ring):
            at = target * depth
            for other in range(HALVES):
                patch = (half ^ other) * ring + target
                for piece in range(pieces):
                    start = pl.multiple_of(patch * width + piece * LANES, LANES)
                    out_ref[at : at + rows, :] = ens_ref[:, pl.ds(start, LANES)]
                    at += rows
            for start in (0, obs - LANES):
                out_ref[at : at + rows, :] = obs_ref[:, start : start + LANES]
                at += rows
            out_ref[at : at + TILE, :] = jnp.zeros((TILE, LANES), F32)
            out_ref[at : at + 1, 0:slots] = list_ref[...].astype(F32)

    return pl.pallas_call(
        kernel,
        out_shape=pltpu.VMEM((ring * depth, LANES), F32),
        in_specs=whole(3),
        out_specs=pl.BlockSpec(memory_space=pltpu.VMEM),
        name="pack",
    )(ensemble, obs_pert, block_list)


def select(listed, slots, weights, own, near_side, far_side):
    members = own.shape[0] - 1
    blocks = own.shape[1] // LANES
    others = slots - FIXED
    ring = lax.axis_size("ring")
    depth = listed.shape[0] // ring
    fixed = (blocks, 2 * blocks - 1)

    def kernel(
        listed_ref, weights_ref, own_ref, near_ref, far_ref, out_ref, scales_ref,
        table, innov_table, lists, staged, wanted, rest, list_sem, sems,
    ):
        region = lax.axis_index("reg")
        offset = (region - 1) * blocks
        odd = lax.rem(region, 2)
        for source in range(ring):
            at = (source + 1) * depth - TILE
            lists[source : source + 1, :] = listed_ref[at : at + 1, :].astype(I32) - offset
        copy = pltpu.make_async_copy(lists, wanted, list_sem)
        copy.start()
        for side, ref in ((1, own_ref), (2 - 2 * odd, near_ref), (2 * odd, far_ref)):
            for block in range(blocks):
                at = side * blocks + block
                table[at] = ref[0:members, block * LANES : (block + 1) * LANES]
                innov_table[at] = ref[members : members + 1, block * LANES : (block + 1) * LANES]
        copy.wait()

        def compact(patch, order):
            count = jnp.int32(0)
            places = [jnp.int32(0)] * FIXED
            for slot in range(slots):
                block = wanted[patch, slot]
                rest[order, count] = block
                if order:
                    rest[2, count] = jnp.int32(slot)
                    places = [jnp.where(block == f, slot, at) for f, at in zip(fixed, places)]
                found = [block == f for f in fixed]
                count = count + jnp.where(found[0] | found[1], 0, 1)
            return places

        copies = []
        for patch in range(ring):
            compact(patch, 0)
            for slot in range(others):
                staged[patch * members : (patch + 1) * members, slot * LANES : (slot + 1) * LANES] = table[rest[0, slot]]
            span = pl.ds(patch * members, members)
            copies.append(pltpu.make_async_copy(staged.at[span], out_ref.at[span], sems.at[patch]))
            copies[-1].start()
        places = compact(lax.axis_index("ring"), 1)
        for slot in range(others):
            scales_ref[slot : slot + 1, :] = innov_table[rest[1, slot]]
            scales_ref[slots + slot : slots + slot + 1, :] = weights_ref[pl.ds(rest[2, slot], 1), :]
        for which in range(FIXED):
            slot = others + which
            scales_ref[slot : slot + 1, :] = innov_table[fixed[which]]
            scales_ref[slots + slot : slots + slot + 1, :] = weights_ref[pl.ds(places[which], 1), :]
        for copy in copies:
            copy.wait()

    return pl.pallas_call(
        kernel,
        out_shape=(
            jax.ShapeDtypeStruct((ring * members, others * LANES), F32),
            pltpu.VMEM((2 * slots, LANES), F32),
        ),
        in_specs=whole(5),
        out_specs=(pl.BlockSpec(memory_space=pl.ANY), pl.BlockSpec(memory_space=pltpu.VMEM)),
        scratch_shapes=[
            pltpu.VMEM((3 * blocks, members, LANES), F32),
            pltpu.VMEM((3 * blocks, 1, LANES), F32),
            pltpu.VMEM((ring, LANES), I32),
            pltpu.VMEM((ring * members, others * LANES), F32),
            pltpu.SMEM((ring, LANES), I32),
            pltpu.SMEM((3, slots), I32),
            pltpu.SemaphoreType.DMA,
            pltpu.SemaphoreType.DMA((ring,)),
        ],
        name="select",
    )(*near(listed, weights, own, near_side, far_side))


def parts(value):
    high = value.astype(BF16)
    return high, (value - high.astype(F32)).astype(BF16)


def product(first, second):
    high1, low1 = first
    high2, low2 = second
    dot = lambda a, b: jnp.dot(a, b, preferred_element_type=F32)
    rows = high1.shape[0] // 2
    done = []
    for at in range(0, high1.shape[0], rows):
        low, high = low1[at : at + rows], high1[at : at + rows]
        both = dot(jnp.concatenate([low, high], axis=0), high2)
        done.append(both[rows:] + (both[0:rows] + dot(high, low2)))
    return jnp.concatenate(done, axis=0)


def scale(block, scales, slot, slots):
    roots = jnp.sqrt(scales[slots + slot : slots + slot + 1, :])
    scaled = block * roots
    return parts(scaled), scaled * (roots * scales[slot : slot + 1, :])


def contract(first, second):
    return lax.dot_general(first, second, (((1,), (1,)), ((), ())), preferred_element_type=F32)


def gram(pieces):
    high, low = (jnp.concatenate(piece, axis=1) for piece in zip(*pieces))
    cross = contract(high, low)
    return contract(high, high) + (cross + cross.T)


def prepare(scales, packed, crossed, rows):
    slots = scales.shape[0] // 2
    ring = lax.axis_size("ring")
    members = HALVES * ring * rows
    depth = packed.shape[0] // ring
    strips = crossed.shape[0] // (ring * rows)
    pieces = strips - FIXED
    width = pieces * LANES

    def kernel(scales_ref, packed_ref, crossed_ref, high_ref, low_ref, mean_ref, gram_ref, drive_ref, columns):
        for source in range(ring):
            for strip in range(strips):
                lanes = slice(strip * LANES, (strip + 1) * LANES)
                skip = strip if strip < pieces else strip + pieces
                own = source * depth + skip * rows
                other = (source * strips + strip) * rows
                at = HALVES * source * rows
                columns[at : at + rows, lanes] = packed_ref[own : own + rows, :]
                columns[at + rows : at + HALVES * rows, lanes] = crossed_ref[other : other + rows, :]
        scales = scales_ref[...]
        made = [
            scale(columns[:, width + which * LANES : width + (which + 1) * LANES], scales, slots - FIXED + which, slots)
            for which in range(FIXED)
        ]
        gram_ref[...] = gram([piece for piece, share in made])
        drive_ref[...] = sum(share for piece, share in made)
        ens = columns[:, 0:width]
        ens_mean = jnp.mean(ens, axis=0, keepdims=True)
        high_ref[...], low_ref[...] = parts(ens - ens_mean)
        mean_ref[...] = jnp.broadcast_to(ens_mean, mean_ref.shape)

    return pl.pallas_call(
        kernel,
        out_shape=(
            pltpu.VMEM((members, width), BF16),
            pltpu.VMEM((members, width), BF16),
            pltpu.VMEM((TILE, width), F32),
            pltpu.VMEM((members, members), F32),
            pltpu.VMEM((members, LANES), F32),
        ),
        in_specs=whole(3),
        out_specs=tuple(whole(5)),
        scratch_shapes=[pltpu.VMEM((members, strips * LANES), F32)],
        name="prepare",
    )(*near(scales, packed, crossed))


def analyse(obs, scales, prepared, rows):
    members, _ = obs.shape
    slots = scales.shape[0] // 2
    groups = members // rows
    ring = groups // HALVES
    width = prepared[0].shape[1]

    def kernel(obs_ref, scales_ref, high_ref, low_ref, mean_ref, gram_ref, drive_ref, out_ref):
        half = lax.axis_index("half")
        scales = scales_ref[...]
        made = [
            scale(obs_ref[:, slot * LANES : (slot + 1) * LANES], scales, slot, slots) for slot in range(slots - FIXED)
        ]
        drive = drive_ref[...] + sum(share for piece, share in made)
        gram_matrix = gram_ref[...] + gram([piece for piece, share in made])
        drive = jnp.sum(drive, axis=1, keepdims=True)
        identity = (
            lax.broadcasted_iota(I32, (members, members), 0) == lax.broadcasted_iota(I32, (members, members), 1)
        ).astype(F32)
        system = identity + gram_matrix / (members - 1.0)
        trace_sum = jnp.sum(system * identity, keepdims=True)
        iterate_y = system / trace_sum
        half_three = 1.5 * identity
        factor = half_three - 0.5 * iterate_y
        y_parts = parts(iterate_y)
        z_parts = parts(factor)
        y_parts = parts(product(y_parts, z_parts))
        for repeat in range(1, NEWTON):
            factor = parts(half_three - 0.5 * product(z_parts, y_parts))
            if repeat < NEWTON - 1:
                iterate_y = product(y_parts, factor)
            iterate_z = product(factor, z_parts)
            if repeat < NEWTON - 1:
                y_parts = parts(iterate_y)
                z_parts = parts(iterate_z)
        root = iterate_z / jnp.sqrt(trace_sum)
        half_step = jnp.sum(root * drive, axis=0, keepdims=True)
        mean_weights = jnp.sum(root * half_step, axis=1, keepdims=True) / (members - 1.0)
        anomalies = (high_ref[...], low_ref[...])
        spread = anomalies[0].astype(F32) + anomalies[1].astype(F32)
        shift = mean_ref[0:1, :] + jnp.sum(mean_weights * spread, axis=0, keepdims=True)
        updated = product(parts(root), anomalies) + shift
        for chunk in range(groups):
            group = (half ^ (chunk % HALVES)) * ring + chunk // HALVES
            at = pl.multiple_of(group * rows, TILE)
            out_ref[pl.ds(at, rows), :] = updated[chunk * rows : (chunk + 1) * rows, :]

    return pl.pallas_call(
        kernel,
        out_shape=pltpu.VMEM((members, width), F32),
        in_specs=whole(7),
        out_specs=pl.BlockSpec(memory_space=pltpu.VMEM),
        name="analyse",
    )(*near(obs, scales, *prepared))


def on_device(ensemble, obs_pert, innovation, block_list, loc_weights):
    regions = lax.axis_size("reg")
    rows, own_obs = obs_pert.shape
    weights = loc_weights.reshape(loc_weights.shape[1:])

    partner = lax.ppermute(obs_pert, "half", [(0, 1), (1, 0)])
    packed = pack(ensemble, obs_pert, block_list)
    packed = lax.all_to_all(packed, "ring", split_axis=0, concat_axis=0, tiled=True)
    table = jnp.concatenate([obs_pert, partner, innovation.reshape(1, own_obs)], axis=0)
    swaps = [[(i + a, i + 1 - a) for i in range(first, regions - 1, 2) for a in (0, 1)] for first in (0, 1)]
    far_side = lax.ppermute(table, "reg", swaps[1])
    near_side = lax.ppermute(table, "reg", swaps[0])
    chosen, scales = select(packed, block_list.shape[1], weights, table, near_side, far_side)
    obs = lax.all_to_all(chosen, "ring", split_axis=0, concat_axis=0, tiled=True)
    ring = lax.axis_size("ring")
    chunks = packed.reshape(ring, -1, LANES)
    part = ensemble.shape[1] // (HALVES * ring) // LANES * rows
    crossed = lax.ppermute(chunks[:, part : chunks.shape[1] - TILE, :].reshape(-1, LANES), "half", [(0, 1), (1, 0)])
    prepared = prepare(scales, packed, crossed, rows)
    updated = analyse(obs, scales, prepared, rows)
    sent = lax.all_to_all(updated, MEM, split_axis=0, concat_axis=0, tiled=True)
    return sent.reshape(sent.shape[0] // rows, rows, -1).transpose(1, 0, 2).reshape(rows, -1)


def solution(mesh):
    groups, regions = (mesh.shape[name] for name in ("mem", "reg"))
    fine = Mesh(mesh.devices.reshape(HALVES, groups // HALVES, regions), MEM + ("reg",))
    return jax.shard_map(
        on_device,
        mesh=fine,
        in_specs=(
            P(MEM, "reg"),
            P(MEM, "reg"),
            P("reg"),
            P(("reg",) + MEM, None),
            P(("reg",) + MEM, None, None),
        ),
        out_specs=P(MEM, "reg"),
        check_vma=False,
    )
```
